256 devices in a mesh: shot: 16 (over y, x), rcv: 16 (over z, core).
Axes of the slice: x: 4, y: 4, z: 8, core: 2. Of those that a mesh axis runs over, the one named last changes fastest.
Arguments:
- estimate: bfloat16 [512, 256, 512], P('shot', 'rcv'), may hold values from -6 to 6
- record: float32 [256, 65536], P('rcv', 'shot'), may hold values from -9 to 9
- fire_times: int32 [512], P('shot'), may hold values from 0 to 65535, as said below
- rcv_delay: int32 [256], P('rcv'), may hold values from 0 to 63, as said below
- threshold: float32 [256], replicated, may hold values from 0.2 to 1.5
Outputs:
- deblended: bfloat16 [512, 256, 512], P('shot', 'rcv')
The draws below stay inside these ranges and needn't reach their ends.
Inputs may be any that keep to these rules, and one draw needn't show every extreme that they name: `fire_times`: shot s fires at a sample from s * 128 to s * 128 + 127; the first shot fires at 0 and the last at the last sample of its range. `rcv_delay`: the first receiver has the largest delay.
All inputs are finite; a program needn't handle non-finite values.
Results may differ from the reference program's by a relative error of at most 0.0068.
Values may be sent and summed in bfloat16 or wider, within the bound.
No kernel may reach another device: no remote copies, remote signals or barrier semaphores. Data moves between devices by JAX's collectives and lax.ppermute only.
A program may use at most 64 MiB of HBM per device.

```python
import math
import jax
import jax.numpy as jnp
from jax import lax

SHOTS = 512
NT = 512
R_DEV = 16
PERIOD = 128
DRIFT = 64
FREQS = 256
RECEIVERS = 256
RECORD = 65536


def draw_fire_times(key, part):
    jitter = jax.random.randint(key, (SHOTS,), 0, PERIOD, dtype=jnp.int32)
    jitter = jitter.at[0].set(0).at[SHOTS - 1].set(PERIOD - 1)
    return jnp.arange(SHOTS, dtype=jnp.int32) * PERIOD + jitter


def draw_rcv_delay(key, part):
    delays = jax.random.randint(jax.random.fold_in(key, 7), (RECEIVERS,), 0, DRIFT, dtype=jnp.int32)
    return delays.at[0].set(DRIFT - 1)


def block_levels(stream_key, shape, shards, least, largest):
    factor_of, own = 1.0, jax.random.fold_in(stream_key, 6)
    for axis_at, blocks in shards:
        heights = jnp.exp(jax.random.uniform(jax.random.fold_in(own, axis_at), (blocks,), jnp.float32, least / len(shards), largest / len(shards)))
        factor_of = factor_of * jnp.repeat(heights, shape[axis_at] // blocks).reshape([-1 if axis == axis_at else 1 for axis in range(len(shape))])
    return factor_of


def normal_values(rng, shape, scale, bound, shards=(), held_as=jnp.bfloat16):
    factor_of = block_levels(rng, shape, shards, -0.22, 0.18) if shards else 1.0
    result = jax.random.normal(rng, shape, jnp.float32) * scale * factor_of
    return jnp.minimum(jnp.maximum(result, -bound), bound).astype(held_as)


def setup_inputs(seed: int = 0) -> dict:
    splits = jax.random.split(jax.random.key(seed), 6)
    estimate = normal_values(splits[0], (SHOTS, RECEIVERS, NT), 1.0, 6.0, ((0, 16), (1, 16)))
    record = normal_values(splits[1], (RECEIVERS, RECORD), 1.5, 9.0, ((0, 16), (1, 16)), jnp.float32)
    fire_times = draw_fire_times(jax.random.fold_in(splits[5], 71), 0)
    rcv_delay = draw_rcv_delay(jax.random.fold_in(splits[5], 71), 0)
    threshold = jnp.clip(jnp.exp(jax.random.uniform(splits[4], (FREQS,), jnp.float32, math.log(0.2), math.log(1.5))), 0.2, 1.5)
    return {"estimate": estimate, "record": record, "fire_times": fire_times, "rcv_delay": rcv_delay, "threshold": threshold}


def time_tables(sample_count):
    freq_count = sample_count // 2
    samples = jnp.arange(sample_count, dtype=jnp.int32)
    freq_ids = jnp.arange(freq_count, dtype=jnp.int32)
    phases = samples[:, None] * freq_ids[None, :] % sample_count
    angles = phases.astype(jnp.float32) * (2.0 * math.pi / sample_count)
    factor = 1.0 / math.sqrt(sample_count)
    cosines = jnp.cos(angles) * factor
    sines = jnp.sin(angles) * factor
    forward = jnp.stack([cosines, -sines], axis=1).astype(jnp.bfloat16)
    weights = jnp.where(freq_ids == 0, 1.0, 2.0).astype(jnp.float32)
    inverse = jnp.stack([(cosines * weights[None, :]).T, (-sines * weights[None, :]).T], axis=0).astype(jnp.bfloat16)
    return (forward, inverse)

def shot_tables(shot_count):
    shot_ids = jnp.arange(shot_count, dtype=jnp.int32)
    phases = shot_ids[:, None] * shot_ids[None, :] % shot_count
    angles = phases.astype(jnp.float32) * (2.0 * math.pi / shot_count)
    factor = 1.0 / math.sqrt(shot_count)
    return ((jnp.cos(angles) * factor).astype(jnp.bfloat16), (jnp.sin(angles) * factor).astype(jnp.bfloat16))

def deblend_block(est_block, record_block, delay_block, fire_times, threshold):
    forward, inverse = time_tables(NT)
    cos_table, sin_table = shot_tables(SHOTS)
    cos_f = cos_table.astype(jnp.float32)
    sin_f = sin_table.astype(jnp.float32)
    spectrum = jnp.einsum('srt,tcf->csrf', est_block.astype(jnp.float32), forward.astype(jnp.float32)).astype(jnp.bfloat16)
    spec_f = spectrum.astype(jnp.float32)
    fk_real = jnp.einsum('ks,srf->krf', cos_f, spec_f[0]) + jnp.einsum('ks,srf->krf', sin_f, spec_f[1])
    fk_imag = jnp.einsum('ks,srf->krf', cos_f, spec_f[1]) - jnp.einsum('ks,srf->krf', sin_f, spec_f[0])
    magnitude = jnp.sqrt(fk_real * fk_real + fk_imag * fk_imag + 1e-12)
    level = threshold[None, None, :]
    factor = jnp.maximum(magnitude - level, 0.0) / jnp.maximum(magnitude, level)
    shrunk_real = (fk_real * factor).astype(jnp.bfloat16).astype(jnp.float32)
    shrunk_imag = (fk_imag * factor).astype(jnp.bfloat16).astype(jnp.float32)
    back_real = jnp.einsum('ks,krf->srf', cos_f, shrunk_real) - jnp.einsum('ks,krf->srf', sin_f, shrunk_imag)
    back_imag = jnp.einsum('ks,krf->srf', sin_f, shrunk_real) + jnp.einsum('ks,krf->srf', cos_f, shrunk_imag)
    back = jnp.stack([back_real, back_imag], axis=0).astype(jnp.bfloat16)
    denoised = jnp.einsum('csrf,cft->srt', back.astype(jnp.float32), inverse.astype(jnp.float32))
    rcv_ids = jnp.arange(delay_block.shape[0], dtype=jnp.int32)
    sample_ids = jnp.arange(NT, dtype=jnp.int32)
    places = ((fire_times[:, None, None] + delay_block[None, :, None] + sample_ids[None, None, :]) % RECORD).astype(jnp.int32)
    predicted = jnp.zeros((delay_block.shape[0], RECORD), jnp.float32).at[rcv_ids[None, :, None], places].add(denoised)
    residual = record_block[rcv_ids[None, :, None], places] - predicted[rcv_ids[None, :, None], places]
    return (denoised + 0.5 * residual).astype(jnp.bfloat16)

def reference(estimate, record, fire_times, rcv_delay, threshold):
    block_total = RECEIVERS // R_DEV

    def one_block(block_id):
        start = (block_id * R_DEV).astype(jnp.int32)
        est_block = lax.dynamic_slice_in_dim(estimate, start, R_DEV, 1)
        record_block = lax.dynamic_slice_in_dim(record, start, R_DEV, 0)
        delay_block = lax.dynamic_slice_in_dim(rcv_delay, start, R_DEV, 0)
        return deblend_block(est_block, record_block, delay_block, fire_times, threshold)
    blocks = lax.map(one_block, jnp.arange(block_total, dtype=jnp.int32))
    return jnp.transpose(blocks, (1, 0, 2, 3)).reshape(SHOTS, RECEIVERS, NT)
```

```python
import math

import jax
import jax.numpy as jnp
import ml_dtypes
import numpy as np
from jax import lax
from jax.experimental import pallas as pl
from jax.experimental.pallas import tpu as pltpu
from jax.sharding import PartitionSpec as P

SHOTS = 512
NT = 512
FREQS = 256
LANES = 128
PERIOD = 128
PARTS = 16
OWN = SHOTS // PARTS
HALF = OWN // 2
BLOCKS = NT // LANES
RIM = 6
PAYLOAD = OWN * (BLOCKS + 1) + 16
VMEM_LIMIT = 48 << 20


def wave(rows, columns, size):
    phases = np.outer(rows, columns) % size
    angles = phases.astype(np.float64) * (2.0 * math.pi / size)
    scale = 1.0 / math.sqrt(size)
    return np.cos(angles) * scale, np.sin(angles) * scale


def rounded(table):
    return np.ascontiguousarray(table).astype(np.float32).astype(ml_dtypes.bfloat16)


def time_tables():
    cosines, sines = wave(np.arange(NT), np.arange(FREQS), NT)
    forward = rounded(np.concatenate([cosines, -sines], axis=1))
    return forward, np.ascontiguousarray(forward.T)


def shot_tables():
    low = np.arange(SHOTS // 2)
    even, odd = np.arange(0, SHOTS, 2), np.arange(1, SHOTS, 2)
    pieces = [np.concatenate(wave(low, part, SHOTS), axis=1) for part in (even, odd)]
    inverse = np.concatenate(wave(np.arange(SHOTS), np.arange(SHOTS), SHOTS), axis=1)
    return rounded(np.stack(pieces)), rounded(inverse)


def swap_table():
    rows = np.arange(256)
    table = np.zeros((256, 256), np.float32)
    table[rows, (rows % 16) * 16 + rows // 16] = 1.0
    return table.astype(ml_dtypes.bfloat16)


def dot(a, b):
    return jnp.dot(a, b, preferred_element_type=jnp.float32)


def pack_kernel(fire_ref, delay_ref, estimate_ref, record_ref, swap_ref, out_ref):
    swap = swap_ref[...]
    estimate = estimate_ref[...].reshape(HALF, 2, PARTS, NT)
    for half in range(2):
        traces = estimate[:, half].reshape(HALF * PARTS, NT)
        turned = dot(swap, traces).astype(jnp.bfloat16).reshape(PARTS, HALF, NT)
        for block in range(BLOCKS):
            first = block * OWN + half * HALF
            out_ref[:, first : first + HALF, :] = turned[:, :, block * LANES : (block + 1) * LANES]
        pieces = [
            record_ref[:, (half * HALF + q) * LANES : (half * HALF + q + 1) * LANES]
            for q in range(HALF)
        ]
        rows = jnp.concatenate(pieces, axis=0).astype(jnp.bfloat16)
        first = BLOCKS * OWN + half * HALF
        out_ref[:, first : first + HALF, :] = (
            dot(swap, rows).astype(jnp.bfloat16).reshape(PARTS, HALF, LANES)
        )
    lane = lax.broadcasted_iota(jnp.int32, (16, LANES), 1)
    offsets = jnp.zeros((16, LANES), jnp.int32)
    for shot in range(OWN):
        offsets = jnp.where(lane == shot, fire_ref[shot] & (PERIOD - 1), offsets)
    first = (BLOCKS + 1) * OWN
    for part in range(PARTS):
        out_ref[part, first : first + 16, :] = (
            (offsets + delay_ref[part]).astype(jnp.float32).astype(jnp.bfloat16)
        )


def main_kernel(
    threshold_ref,
    data_ref,
    forward_ref,
    inverse_ref,
    split_ref,
    full_ref,
    out_ref,
    stack_ref,
    shrunk_ref,
    denoised_ref,
    offset_ref,
    placed_ref,
    difference_ref,
):
    half_shots = SHOTS // 2
    data = data_ref
    lane = lax.broadcasted_iota(jnp.int32, (OWN, LANES), 1)
    row = lax.broadcasted_iota(jnp.int32, (OWN, LANES), 0)
    first = (BLOCKS + 1) * OWN
    picked = []
    for part in range(PARTS):
        rows = data[part, first : first + 16, :].astype(jnp.float32)
        rows = jnp.concatenate([rows, rows], axis=0)
        picked.append(jnp.where(lane == row, rows, 0.0).astype(jnp.bfloat16))
    ones = jnp.ones((LANES, LANES), jnp.bfloat16)
    offset_ref[...] = dot(jnp.concatenate(picked, axis=0), ones).astype(jnp.int32)

    waves = []
    for half in range(2):
        traces = jnp.concatenate(
            [
                data[:, block * OWN + half * HALF : block * OWN + (half + 1) * HALF, :].reshape(
                    half_shots, LANES
                )
                for block in range(BLOCKS)
            ],
            axis=1,
        )
        spectrum = dot(traces, forward_ref[...]).astype(jnp.bfloat16)
        stack_ref[half, :half_shots, :] = spectrum
        stack_ref[half, half_shots:, :FREQS] = spectrum[:, FREQS:]
        stack_ref[half, half_shots:, FREQS:] = -spectrum[:, :FREQS]
        waves.append(dot(split_ref[half], stack_ref[half]))

    freq = lax.broadcasted_iota(jnp.int32, (1, FREQS), 1)
    weight = jnp.where(freq == 0, 1.0, 2.0).astype(jnp.float32)
    level = weight * threshold_ref[...]
    for half in range(2):
        fk = waves[0] + waves[1] if half == 0 else waves[0] - waves[1]
        real, imag = fk[:, :FREQS], fk[:, FREQS:]
        power = real * real + imag * imag + 1e-12
        factor = jnp.maximum(weight - level * lax.rsqrt(power), 0.0)
        real = (real * factor).astype(jnp.bfloat16)
        imag = (imag * factor).astype(jnp.bfloat16)
        here = slice(half * half_shots, (half + 1) * half_shots)
        there = slice(SHOTS + half * half_shots, SHOTS + (half + 1) * half_shots)
        shrunk_ref[here, :FREQS] = real
        shrunk_ref[here, FREQS:] = imag
        shrunk_ref[there, :FREQS] = -imag
        shrunk_ref[there, FREQS:] = real

    back = dot(full_ref[...], shrunk_ref[...]).astype(jnp.bfloat16)
    denoised_ref[...] = dot(back, inverse_ref[...])

    step = OWN
    zero = jnp.zeros((step, LANES), jnp.float32)

    def rotated(value, index):
        return jnp.take_along_axis(value, index, axis=1, mode="promise_in_bounds")

    for start in range(0, SHOTS, step):
        offset = offset_ref[start : start + step, :]
        index = (lane - offset) & (LANES - 1)
        near, far = lane >= offset, lane >= offset - LANES
        turned = [
            rotated(
                denoised_ref[start : start + step, block * LANES : (block + 1) * LANES], index
            )
            for block in range(BLOCKS)
        ]
        turned = [zero, zero] + turned + [zero, zero]
        for piece in range(RIM):
            placed_ref[piece, 8 + start : 8 + start + step, :] = jnp.where(
                near, turned[piece + 2], jnp.where(far, turned[piece + 1], turned[piece])
            )
    for piece in range(1, RIM):
        placed_ref[piece, 0:8, :] = placed_ref[piece, SHOTS : SHOTS + 8, :]

    for start in range(0, SHOTS, step):
        total = placed_ref[0, 8 + start : 8 + start + step, :]
        for piece in range(1, RIM):
            total = total + placed_ref[piece, 8 + start - piece : 8 + start - piece + step, :]
        record = data[start // step, BLOCKS * OWN : BLOCKS * OWN + step, :].astype(jnp.float32)
        difference_ref[start : start + step, :] = 0.5 * (record - total)
    difference_ref[SHOTS : SHOTS + 8, :] = difference_ref[0:8, :]

    for start in range(0, SHOTS, step):
        offset = offset_ref[start : start + step, :]
        index = (lane + offset) & (LANES - 1)
        near, far = lane >= offset, lane >= offset - LANES
        rows = [difference_ref[start + piece : start + piece + step, :] for piece in range(RIM)]
        rows[0] = jnp.where(near, rows[0], rows[4])
        rows[1] = jnp.where(far, rows[1], rows[5])
        turned = [rotated(rows[block], index) for block in range(BLOCKS)]
        reach = lane + offset
        one, two = reach >= LANES, reach >= 2 * LANES
        for block in range(BLOCKS):
            residual = jnp.where(
                two,
                turned[(block + 2) % BLOCKS],
                jnp.where(one, turned[(block + 1) % BLOCKS], turned[block]),
            )
            lanes = slice(block * LANES, (block + 1) * LANES)
            out_ref[start : start + step, lanes] = (
                denoised_ref[start : start + step, lanes] + residual
            ).astype(jnp.bfloat16)


def unpack_kernel(data_ref, swap_ref, out_ref):
    swap = swap_ref[...]
    for half in range(2):
        rows = data_ref[:, half * HALF : (half + 1) * HALF, :].reshape(PARTS * HALF, NT)
        out_ref[half * HALF : (half + 1) * HALF] = (
            dot(swap, rows).astype(jnp.bfloat16).reshape(HALF, PARTS, NT)
        )


def vmem():
    return pl.BlockSpec(memory_space=pltpu.VMEM)


def smem():
    return pl.BlockSpec(memory_space=pltpu.SMEM)


PARAMS = pltpu.CompilerParams(vmem_limit_bytes=VMEM_LIMIT)


def shards(estimate, record, fire_times, rcv_delay, threshold):
    forward, inverse = time_tables()
    split, full = shot_tables()
    swap = jnp.asarray(swap_table())
    packed = pl.pallas_call(
        pack_kernel,
        out_shape=jax.ShapeDtypeStruct((PARTS, PAYLOAD, LANES), jnp.bfloat16),
        in_specs=[smem(), smem(), vmem(), vmem(), vmem()],
        out_specs=vmem(),
        compiler_params=PARAMS,
        name="pack",
    )(fire_times, rcv_delay, estimate, record, swap)
    gathered = lax.all_to_all(packed, "shot", split_axis=0, concat_axis=0, tiled=True)
    updated = pl.pallas_call(
        main_kernel,
        out_shape=jax.ShapeDtypeStruct((SHOTS, NT), jnp.bfloat16),
        in_specs=[vmem()] * 6,
        out_specs=vmem(),
        scratch_shapes=[
            pltpu.VMEM((2, SHOTS, NT), jnp.bfloat16),
            pltpu.VMEM((2 * SHOTS, NT), jnp.bfloat16),
            pltpu.VMEM((SHOTS, NT), jnp.float32),
            pltpu.VMEM((SHOTS, LANES), jnp.int32),
            pltpu.VMEM((RIM, SHOTS + 8, LANES), jnp.float32),
            pltpu.VMEM((SHOTS + 8, LANES), jnp.float32),
        ],
        compiler_params=PARAMS,
        name="main",
    )(
        threshold.reshape(1, FREQS),
        gathered,
        jnp.asarray(forward),
        jnp.asarray(inverse),
        jnp.asarray(split),
        jnp.asarray(full),
    )
    returned = lax.all_to_all(
        updated.reshape(PARTS, OWN, NT), "shot", split_axis=0, concat_axis=0, tiled=True
    )
    return pl.pallas_call(
        unpack_kernel,
        out_shape=jax.ShapeDtypeStruct((OWN, PARTS, NT), jnp.bfloat16),
        in_specs=[vmem()] * 2,
        out_specs=vmem(),
        compiler_params=PARAMS,
        name="unpack",
    )(returned, swap)


def solution(mesh):
    in_specs = (P("shot", "rcv", None), P("rcv", "shot"), P("shot"), P("rcv"), P())
    out_specs = P("shot", "rcv", None)
    return jax.shard_map(shards, mesh=mesh, in_specs=in_specs, out_specs=out_specs, check_vma=False)
```

```python
import math

import jax
import jax.numpy as jnp
import ml_dtypes
import numpy as np
from jax import lax
from jax.experimental import pallas as pl
from jax.experimental.pallas import tpu as pltpu
from jax.sharding import PartitionSpec as P

SHOTS = 512
NT = 512
FREQS = 256
LANES = 128
PERIOD = 128
PARTS = 16
OWN = SHOTS // PARTS
HALF = OWN // 2
BLOCKS = NT // LANES
RIM = 6
PAYLOAD = OWN * (BLOCKS + 1) + 8
VMEM_LIMIT = 48 << 20


def wave(rows, columns, size):
    phases = np.outer(rows, columns) % size
    angles = phases.astype(np.float64) * (2.0 * math.pi / size)
    scale = 1.0 / math.sqrt(size)
    return np.cos(angles) * scale, np.sin(angles) * scale


def rounded(table):
    return np.ascontiguousarray(table).astype(np.float32).astype(ml_dtypes.bfloat16)


def time_tables():
    cosines, sines = wave(np.arange(NT), np.arange(FREQS), NT)
    forward = rounded(np.concatenate([cosines, -sines], axis=1))
    return forward, np.ascontiguousarray(forward.T)


def shot_tables():
    low = np.arange(SHOTS // 2)
    even, odd = np.arange(0, SHOTS, 2), np.arange(1, SHOTS, 2)
    pieces = [np.concatenate(wave(low, part, SHOTS), axis=1) for part in (even, odd)]
    inverse = np.concatenate(wave(np.arange(SHOTS), np.arange(SHOTS), SHOTS), axis=1)
    return rounded(np.stack(pieces)), rounded(inverse)


def dot(a, b):
    return jnp.dot(a, b, preferred_element_type=jnp.float32)


def swap_table():
    row = lax.broadcasted_iota(jnp.int32, (256, 256), 0)
    column = lax.broadcasted_iota(jnp.int32, (256, 256), 1)
    source = (row & 15) * 16 + (row >> 4)
    return jnp.where(column == source, 1.0, 0.0).astype(jnp.bfloat16)


def pack_kernel(
    fire_hbm,
    delay_hbm,
    estimate_hbm,
    record_hbm,
    out_ref,
    fire_ref,
    delay_ref,
    estimate_ref,
    record_ref,
    small_sems,
    trace_sems,
    record_sem,
):
    halves = []
    for half in range(2):
        halves.append(
            pltpu.make_async_copy(
                estimate_hbm.at[:, half], estimate_ref.at[half], trace_sems.at[half]
            )
        )
        halves[-1].start()
    whole = pltpu.make_async_copy(record_hbm, record_ref, record_sem)
    whole.start()
    fires = pltpu.make_async_copy(fire_hbm, fire_ref, small_sems.at[0])
    delays = pltpu.make_async_copy(delay_hbm, delay_ref, small_sems.at[1])
    fires.start()
    delays.start()
    swap = swap_table()
    lane = lax.broadcasted_iota(jnp.int32, (8, LANES), 1)
    offsets = jnp.zeros((8, LANES), jnp.int32)
    fires.wait()
    delays.wait()
    for shot in range(OWN):
        offsets = jnp.where(lane == shot, fire_ref[shot] & (PERIOD - 1), offsets)
    first = (BLOCKS + 1) * OWN
    for part in range(PARTS):
        out_ref[part, first : first + 8, :] = (
            (offsets + delay_ref[part]).astype(jnp.float32).astype(jnp.bfloat16)
        )
    for half in range(2):
        halves[half].wait()
        turned = dot(swap, estimate_ref[half].reshape(HALF * PARTS, NT)).astype(jnp.bfloat16)
        turned = turned.reshape(PARTS, HALF, NT)
        for block in range(BLOCKS):
            first = block * OWN + half * HALF
            out_ref[:, first : first + HALF, :] = turned[:, :, block * LANES : (block + 1) * LANES]
    whole.wait()
    for half in range(2):
        pieces = [
            record_ref[:, (half * HALF + q) * LANES : (half * HALF + q + 1) * LANES]
            for q in range(HALF)
        ]
        rows = jnp.concatenate(pieces, axis=0).astype(jnp.bfloat16)
        first = BLOCKS * OWN + half * HALF
        out_ref[:, first : first + HALF, :] = (
            dot(swap, rows).astype(jnp.bfloat16).reshape(PARTS, HALF, LANES)
        )


def main_kernel(
    threshold_hbm,
    data_ref,
    forward_ref,
    inverse_ref,
    split_ref,
    full_ref,
    out_ref,
    stack_ref,
    shrunk_ref,
    denoised_ref,
    offset_ref,
    placed_ref,
    difference_ref,
    threshold_ref,
    threshold_sem,
):
    fetch = pltpu.make_async_copy(threshold_hbm, threshold_ref, threshold_sem)
    fetch.start()
    half_shots = SHOTS // 2
    data = data_ref
    lane = lax.broadcasted_iota(jnp.int32, (OWN, LANES), 1)
    row = lax.broadcasted_iota(jnp.int32, (OWN, LANES), 0)
    first = (BLOCKS + 1) * OWN
    picked = []
    for part in range(PARTS):
        rows = data[part, first : first + 8, :].astype(jnp.float32)
        rows = jnp.concatenate([rows] * 4, axis=0)
        picked.append(jnp.where(lane == row, rows, 0.0).astype(jnp.bfloat16))
    ones = jnp.ones((LANES, LANES), jnp.bfloat16)
    offset_ref[...] = dot(jnp.concatenate(picked, axis=0), ones).astype(jnp.int32)

    waves = []
    for half in range(2):
        traces = jnp.concatenate(
            [
                data[:, block * OWN + half * HALF : block * OWN + (half + 1) * HALF, :].reshape(
                    half_shots, LANES
                )
                for block in range(BLOCKS)
            ],
            axis=1,
        )
        spectrum = dot(traces, forward_ref[...]).astype(jnp.bfloat16)
        stack_ref[half, :half_shots, :] = spectrum
        stack_ref[half, half_shots:, :FREQS] = spectrum[:, FREQS:]
        stack_ref[half, half_shots:, FREQS:] = -spectrum[:, :FREQS]
        waves.append(dot(split_ref[half], stack_ref[half]))

    freq = lax.broadcasted_iota(jnp.int32, (1, FREQS), 1)
    weight = jnp.where(freq == 0, 1.0, 2.0).astype(jnp.float32)
    fetch.wait()
    level = weight * threshold_ref[...]
    for half in range(2):
        fk = waves[0] + waves[1] if half == 0 else waves[0] - waves[1]
        real, imag = fk[:, :FREQS], fk[:, FREQS:]
        power = real * real + imag * imag + 1e-12
        factor = jnp.maximum(weight - level * lax.rsqrt(power), 0.0)
        real = (real * factor).astype(jnp.bfloat16)
        imag = (imag * factor).astype(jnp.bfloat16)
        here = slice(half * half_shots, (half + 1) * half_shots)
        there = slice(SHOTS + half * half_shots, SHOTS + (half + 1) * half_shots)
        shrunk_ref[here, :FREQS] = real
        shrunk_ref[here, FREQS:] = imag
        shrunk_ref[there, :FREQS] = -imag
        shrunk_ref[there, FREQS:] = real

    back = dot(full_ref[...], shrunk_ref[...]).astype(jnp.bfloat16)
    denoised_ref[...] = dot(back, inverse_ref[...])

    step = OWN
    zero = jnp.zeros((step, LANES), jnp.float32)

    def rotated(value, index):
        return jnp.take_along_axis(value, index, axis=1, mode="promise_in_bounds")

    for start in range(0, SHOTS, step):
        offset = offset_ref[start : start + step, :]
        index = (lane - offset) & (LANES - 1)
        near, far = lane >= offset, lane >= offset - LANES
        turned = [
            rotated(
                denoised_ref[start : start + step, block * LANES : (block + 1) * LANES], index
            )
            for block in range(BLOCKS)
        ]
        turned = [zero, zero] + turned + [zero, zero]
        for piece in range(RIM):
            placed_ref[piece, 8 + start : 8 + start + step, :] = jnp.where(
                near, turned[piece + 2], jnp.where(far, turned[piece + 1], turned[piece])
            )
    for piece in range(1, RIM):
        placed_ref[piece, 0:8, :] = placed_ref[piece, SHOTS : SHOTS + 8, :]

    for start in range(0, SHOTS, step):
        total = placed_ref[0, 8 + start : 8 + start + step, :]
        for piece in range(1, RIM):
            total = total + placed_ref[piece, 8 + start - piece : 8 + start - piece + step, :]
        record = data[start // step, BLOCKS * OWN : BLOCKS * OWN + step, :].astype(jnp.float32)
        difference_ref[start : start + step, :] = 0.5 * (record - total)
    difference_ref[SHOTS : SHOTS + 8, :] = difference_ref[0:8, :]

    for start in range(0, SHOTS, step):
        offset = offset_ref[start : start + step, :]
        index = (lane + offset) & (LANES - 1)
        near, far = lane >= offset, lane >= offset - LANES
        rows = [difference_ref[start + piece : start + piece + step, :] for piece in range(RIM)]
        rows[0] = jnp.where(near, rows[0], rows[4])
        rows[1] = jnp.where(far, rows[1], rows[5])
        turned = [rotated(rows[block], index) for block in range(BLOCKS)]
        reach = lane + offset
        one, two = reach >= LANES, reach >= 2 * LANES
        for block in range(BLOCKS):
            residual = jnp.where(
                two,
                turned[(block + 2) % BLOCKS],
                jnp.where(one, turned[(block + 1) % BLOCKS], turned[block]),
            )
            lanes = slice(block * LANES, (block + 1) * LANES)
            out_ref[start : start + step, lanes] = (
                denoised_ref[start : start + step, lanes] + residual
            ).astype(jnp.bfloat16)


def unpack_kernel(data_ref, out_hbm, out_ref, sems):
    swap = swap_table()
    width = NT // 2
    copies = []
    for half in range(2):
        shots = slice(half * HALF, (half + 1) * HALF)
        for side in range(2):
            lanes = slice(side * width, (side + 1) * width)
            rows = data_ref[:, shots, lanes].reshape(PARTS * HALF, width)
            out_ref[shots, :, lanes] = (
                dot(swap, rows).astype(jnp.bfloat16).reshape(HALF, PARTS, width)
            )
            place = (pl.ds(half * HALF, HALF), slice(None), pl.ds(side * width, width))
            copies.append(
                pltpu.make_async_copy(
                    out_ref.at[place], out_hbm.at[place], sems.at[2 * half + side]
                )
            )
            copies[-1].start()
    for copy in copies:
        copy.wait()


def vmem():
    return pl.BlockSpec(memory_space=pltpu.VMEM)


def hbm():
    return pl.BlockSpec(memory_space=pltpu.HBM)


def kept(value):
    return pltpu.with_memory_space_constraint(value, pltpu.HBM)


PARAMS = pltpu.CompilerParams(vmem_limit_bytes=VMEM_LIMIT)


def shards(estimate, record, fire_times, rcv_delay, threshold):
    forward, inverse = time_tables()
    split, full = shot_tables()
    packed = pl.pallas_call(
        pack_kernel,
        out_shape=jax.ShapeDtypeStruct((PARTS, PAYLOAD, LANES), jnp.bfloat16),
        in_specs=[hbm()] * 4,
        out_specs=vmem(),
        scratch_shapes=[
            pltpu.SMEM((OWN,), jnp.int32),
            pltpu.SMEM((PARTS,), jnp.int32),
            pltpu.VMEM((2, HALF, PARTS, NT), jnp.bfloat16),
            pltpu.VMEM((PARTS, OWN * LANES), jnp.float32),
            pltpu.SemaphoreType.DMA((2,)),
            pltpu.SemaphoreType.DMA((2,)),
            pltpu.SemaphoreType.DMA,
        ],
        compiler_params=PARAMS,
        name="pack",
    )(
        kept(fire_times),
        kept(rcv_delay),
        kept(estimate.reshape(HALF, 2, PARTS, NT)),
        kept(record),
    )
    gathered = lax.all_to_all(packed, "shot", split_axis=0, concat_axis=0, tiled=True)
    updated = pl.pallas_call(
        main_kernel,
        out_shape=jax.ShapeDtypeStruct((SHOTS, NT), jnp.bfloat16),
        in_specs=[hbm()] + [vmem()] * 5,
        out_specs=vmem(),
        scratch_shapes=[
            pltpu.VMEM((2, SHOTS, NT), jnp.bfloat16),
            pltpu.VMEM((2 * SHOTS, NT), jnp.bfloat16),
            pltpu.VMEM((SHOTS, NT), jnp.float32),
            pltpu.VMEM((SHOTS, LANES), jnp.int32),
            pltpu.VMEM((RIM, SHOTS + 8, LANES), jnp.float32),
            pltpu.VMEM((SHOTS + 8, LANES), jnp.float32),
            pltpu.VMEM((1, FREQS), jnp.float32),
            pltpu.SemaphoreType.DMA,
        ],
        compiler_params=PARAMS,
        name="main",
    )(
        kept(threshold.reshape(1, FREQS)),
        gathered,
        jnp.asarray(forward),
        jnp.asarray(inverse),
        jnp.asarray(split),
        jnp.asarray(full),
    )
    returned = lax.all_to_all(
        updated.reshape(PARTS, OWN, NT), "shot", split_axis=0, concat_axis=0, tiled=True
    )
    return pl.pallas_call(
        unpack_kernel,
        out_shape=jax.ShapeDtypeStruct((OWN, PARTS, NT), jnp.bfloat16),
        in_specs=[vmem()],
        out_specs=hbm(),
        scratch_shapes=[
            pltpu.VMEM((OWN, PARTS, NT), jnp.bfloat16),
            pltpu.SemaphoreType.DMA((4,)),
        ],
        compiler_params=PARAMS,
        name="unpack",
    )(returned)


def solution(mesh):
    in_specs = (P("shot", "rcv", None), P("rcv", "shot"), P("shot"), P("rcv"), P())
    out_specs = P("shot", "rcv", None)
    return jax.shard_map(shards, mesh=mesh, in_specs=in_specs, out_specs=out_specs, check_vma=False)
```

```python
import math

import jax
import jax.numpy as jnp
import ml_dtypes
import numpy as np
from jax import lax
from jax.experimental import pallas as pl
from jax.experimental.pallas import tpu as pltpu
from jax.sharding import PartitionSpec as P

SHOTS = 512
NT = 512
FREQS = 256
LANES = 128
PERIOD = 128
PARTS = 16
OWN = SHOTS // PARTS
HALF = OWN // 2
BLOCKS = NT // LANES
RIM = 6
PAYLOAD = OWN * BLOCKS + 8
CHUNKS = 2
VMEM_LIMIT = 24 << 20


def wave(rows, columns, size):
    phases = np.outer(rows, columns) % size
    angles = phases.astype(np.float64) * (2.0 * math.pi / size)
    scale = 1.0 / math.sqrt(size)
    return np.cos(angles) * scale, np.sin(angles) * scale


def rounded(table):
    return np.ascontiguousarray(table).astype(np.float32).astype(ml_dtypes.bfloat16)


def tables():
    low = np.arange(SHOTS // 2)
    even, odd = np.arange(0, SHOTS, 2), np.arange(1, SHOTS, 2)
    pieces = [np.concatenate(wave(low, part, SHOTS), axis=1) for part in (even, odd)]
    inverse = np.concatenate(wave(np.arange(SHOTS), np.arange(SHOTS), SHOTS), axis=1)
    return rounded(np.stack(pieces)), rounded(inverse)


def dot(a, b):
    return jnp.dot(a, b, preferred_element_type=jnp.float32)


def swap_table():
    row = lax.broadcasted_iota(jnp.int32, (256, 256), 0)
    column = lax.broadcasted_iota(jnp.int32, (256, 256), 1)
    source = (row & 15) * 16 + (row >> 4)
    return jnp.where(column == source, 1.0, 0.0).astype(jnp.bfloat16)


def pack_kernel(
    fire_hbm,
    delay_hbm,
    estimate_hbm,
    record_hbm,
    out_ref,
    fire_ref,
    delay_ref,
    estimate_ref,
    record_ref,
    small_sems,
    in_sems,
):
    pieces = [(half, 0) for half in range(2)]
    width = NT
    arrivals = []
    for at, (half, side) in enumerate(pieces):
        arrivals.append(
            pltpu.make_async_copy(
                estimate_hbm.at[:, half],
                estimate_ref.at[half],
                in_sems.at[at],
            )
        )
    fires = pltpu.make_async_copy(fire_hbm, fire_ref, small_sems.at[0])
    delays = pltpu.make_async_copy(delay_hbm, delay_ref, small_sems.at[1])
    heads = pltpu.make_async_copy(
        record_hbm.at[:, pl.ds(0, RIM * LANES)], record_ref, small_sems.at[2]
    )
    arrivals[0].start()
    fires.start()
    delays.start()
    heads.start()
    for arrival in arrivals[1:]:
        arrival.start()
    swap = swap_table()
    def turn(at):
        half, side = pieces[at]
        arrivals[at].wait()
        traces = estimate_ref[half]
        turned = dot(swap, traces.reshape(HALF * PARTS, width)).astype(jnp.bfloat16)
        turned = turned.reshape(PARTS, HALF, width)
        for block in range(4):
            first = (4 * half + block) * HALF
            out_ref[:, first : first + HALF, :] = turned[:, :, block * LANES : (block + 1) * LANES]

    turn(0)
    lane = lax.broadcasted_iota(jnp.int32, (8, LANES), 1)
    row = lax.broadcasted_iota(jnp.int32, (8, LANES), 0)
    offsets = jnp.zeros((8, LANES), jnp.int32)
    fires.wait()
    delays.wait()
    for shot in range(OWN):
        offsets = jnp.where(lane == shot, fire_ref[shot] & (PERIOD - 1), offsets)
    heads.wait()
    for part in range(PARTS):
        rows = (offsets + delay_ref[part]).astype(jnp.float32)
        for piece in range(RIM):
            head = record_ref[part : part + 1, piece * LANES : (piece + 1) * LANES]
            rows = jnp.where(row == piece, jnp.broadcast_to(head, (8, LANES)), rows)
        out_ref[part, BLOCKS * OWN : BLOCKS * OWN + 8, :] = rows.astype(jnp.bfloat16)
    turn(1)


def rotated(value, index):
    return jnp.take_along_axis(value, index, axis=1, mode="promise_in_bounds")


def read_windows(rows, offset, lane):
    near, far = lane >= offset, lane >= offset - LANES
    reach = lane + offset
    one, two = reach >= LANES, reach >= 2 * LANES
    rows = [jnp.where(near, rows[0], rows[4]), jnp.where(far, rows[1], rows[5]), *rows[2:4]]
    turned = [rotated(row, reach & (LANES - 1)) for row in rows]
    return [
        jnp.where(
            two,
            turned[(block + 2) % BLOCKS],
            jnp.where(one, turned[(block + 1) % BLOCKS], turned[block]),
        )
        for block in range(BLOCKS)
    ]


def main_kernel(
    threshold_hbm,
    fire_hbm,
    delay_hbm,
    record_hbm,
    data_ref,
    split_ref,
    full_ref,
    out_ref,
    window_ref,
    stack_ref,
    shrunk_ref,
    denoised_ref,
    offset_ref,
    placed_ref,
    difference_ref,
    threshold_ref,
    fire_ref,
    delay_ref,
    record_ref,
    sems,
):
    pairs = [
        (threshold_hbm, threshold_ref),
        (fire_hbm, fire_ref),
        (delay_hbm, delay_ref),
        (record_hbm, record_ref),
    ]
    fetches = [
        pltpu.make_async_copy(source, target, sems.at[at])
        for at, (source, target) in enumerate(pairs)
    ]
    for fetch in fetches:
        fetch.start()
    half_shots = SHOTS // 2
    data = data_ref
    lane = lax.broadcasted_iota(jnp.int32, (OWN, LANES), 1)
    row = lax.broadcasted_iota(jnp.int32, (OWN, LANES), 0)

    waves = []
    for half in range(2):
        traces = jnp.concatenate(
            [
                data[:, first : first + HALF, :].reshape(half_shots, LANES)
                for first in range(half * BLOCKS * HALF, (half + 1) * BLOCKS * HALF, HALF)
            ],
            axis=1,
        )
        real = dot(traces, full_ref[:, :FREQS]).astype(jnp.bfloat16)
        imag = (-dot(traces, full_ref[:, SHOTS : SHOTS + FREQS])).astype(jnp.bfloat16)
        stack_ref[half, :half_shots, :FREQS] = real
        stack_ref[half, :half_shots, FREQS:] = imag
        stack_ref[half, half_shots:, :FREQS] = imag
        stack_ref[half, half_shots:, FREQS:] = -real
        waves.append(dot(split_ref[half], stack_ref[half]))

    first = BLOCKS * OWN
    picked = []
    for part in range(PARTS):
        rows = data[part, first : first + 8, :].astype(jnp.float32)
        rows = jnp.broadcast_to(rows[7:8, :], (OWN, LANES))
        picked.append(jnp.where(lane == row, rows, 0.0).astype(jnp.bfloat16))
    ones = jnp.ones((LANES, LANES), jnp.bfloat16)
    offset_ref[...] = dot(jnp.concatenate(picked, axis=0), ones).astype(jnp.int32)

    for fetch in fetches:
        fetch.wait()
    freq = lax.broadcasted_iota(jnp.int32, (1, FREQS), 1)
    weight = jnp.where(freq == 0, 1.0, 2.0).astype(jnp.float32)
    level = weight * threshold_ref[...]
    for half in range(2):
        fk = waves[0] + waves[1] if half == 0 else waves[0] - waves[1]
        real, imag = fk[:, :FREQS], fk[:, FREQS:]
        power = real * real + imag * imag + 1e-12
        factor = jnp.maximum(weight - level * lax.rsqrt(power), 0.0)
        less = (-imag * factor).astype(jnp.bfloat16)
        real = (real * factor).astype(jnp.bfloat16)
        here = slice(half * half_shots, (half + 1) * half_shots)
        there = slice(SHOTS + half * half_shots, SHOTS + (half + 1) * half_shots)
        shrunk_ref[here, :FREQS] = real
        shrunk_ref[there, :FREQS] = less
        shrunk_ref[here, FREQS:] = less
        shrunk_ref[there, FREQS:] = -real

    wide = lax.broadcasted_iota(jnp.int32, (PARTS, LANES), 1)
    which = lax.broadcasted_iota(jnp.int32, (PARTS, LANES), 0)
    delay = jnp.zeros((PARTS, LANES), jnp.int32)
    for part in range(PARTS):
        delay = jnp.where(which == part, delay_ref[part], delay)

    def record_window(shot):
        rows = [
            record_ref[:, piece * LANES : (piece + 1) * LANES]
            if RIM <= piece < OWN
            else jnp.zeros((PARTS, LANES), jnp.float32)
            for piece in range(shot, shot + RIM)
        ]
        offset = delay + (fire_ref[shot] & (PERIOD - 1))
        for block, value in enumerate(read_windows(rows, offset, wide)):
            window_ref[shot, :, block * LANES : (block + 1) * LANES] = 0.5 * value

    step = OWN
    zero = jnp.zeros((step, LANES), jnp.float32)

    def place(start):
        offset = offset_ref[start : start + step, :]
        index = (lane - offset) & (LANES - 1)
        near, far = lane >= offset, lane >= offset - LANES
        turned = [
            rotated(
                denoised_ref[start : start + step, block * LANES : (block + 1) * LANES], index
            )
            for block in range(BLOCKS)
        ]
        turned = [zero, zero] + turned + [zero, zero]
        for piece in range(RIM):
            placed_ref[piece, 8 + start : 8 + start + step, :] = jnp.where(
                near, turned[piece + 2], jnp.where(far, turned[piece + 1], turned[piece])
            )

    def subtract(start):
        total = placed_ref[0, 8 + start : 8 + start + step, :]
        for piece in range(1, RIM):
            total = total + placed_ref[piece, 8 + start - piece : 8 + start - piece + step, :]
        difference_ref[start : start + step, :] = -0.5 * total
        heads = data[start // step, BLOCKS * OWN : BLOCKS * OWN + 8, :].astype(jnp.float32)
        heads = jnp.where(row[:8] < RIM, 0.5 * heads, 0.0)
        difference_ref[start : start + 8, :] = difference_ref[start : start + 8, :] + heads

    def finish(start):
        offset = offset_ref[start : start + step, :]
        rows = [difference_ref[start + piece : start + piece + step, :] for piece in range(RIM)]
        for block, value in enumerate(read_windows(rows, offset, lane)):
            lanes = slice(block * LANES, (block + 1) * LANES)
            out_ref[start : start + step, lanes] = (
                denoised_ref[start : start + step, lanes] + value
            ).astype(jnp.bfloat16)

    inverse = jnp.concatenate([full_ref[:FREQS, :SHOTS], full_ref[:FREQS, SHOTS:]], axis=0)
    part_shots = SHOTS // CHUNKS
    for part in range(CHUNKS):
        shots = slice(part * part_shots, (part + 1) * part_shots)
        back = dot(full_ref[shots, :], shrunk_ref[...]).astype(jnp.bfloat16)
        denoised_ref[shots, :] = dot(back, inverse)
        for shot in range(part * OWN // CHUNKS, (part + 1) * OWN // CHUNKS):
            record_window(shot)
        for start in range(part * part_shots, (part + 1) * part_shots, step):
            place(start)
    for piece in range(1, RIM):
        placed_ref[piece, 0:8, :] = placed_ref[piece, SHOTS : SHOTS + 8, :]
    for start in range(0, SHOTS, step):
        subtract(start)
    difference_ref[SHOTS : SHOTS + 8, :] = difference_ref[0:8, :]
    for start in range(0, SHOTS, step):
        finish(start)


def unpack_kernel(data_ref, window_ref, out_hbm, out_ref, sems):
    swap = swap_table()
    width = NT // 2
    copies = []
    for half in range(2):
        shots = slice(half * HALF, (half + 1) * HALF)
        for side in range(2):
            lanes = slice(side * width, (side + 1) * width)
            rows = data_ref[:, shots, lanes].reshape(PARTS * HALF, width)
            out_ref[shots, :, lanes] = (
                dot(swap, rows).reshape(HALF, PARTS, width) + window_ref[shots, :, lanes]
            ).astype(jnp.bfloat16)
            place = (pl.ds(half * HALF, HALF), slice(None), pl.ds(side * width, width))
            copies.append(
                pltpu.make_async_copy(
                    out_ref.at[place], out_hbm.at[place], sems.at[2 * half + side]
                )
            )
            copies[-1].start()
    for copy in copies:
        copy.wait()


def vmem():
    return pl.BlockSpec(memory_space=pltpu.VMEM)


def hbm():
    return pl.BlockSpec(memory_space=pltpu.HBM)


def kept(value):
    return pltpu.with_memory_space_constraint(value, pltpu.HBM)


PARAMS = pltpu.CompilerParams(vmem_limit_bytes=VMEM_LIMIT)


def shards(estimate, record, fire_times, rcv_delay, threshold):
    packed = pl.pallas_call(
        pack_kernel,
        out_shape=jax.ShapeDtypeStruct((PARTS, PAYLOAD, LANES), jnp.bfloat16),
        in_specs=[hbm()] * 4,
        out_specs=vmem(),
        scratch_shapes=[
            pltpu.SMEM((OWN,), jnp.int32),
            pltpu.SMEM((PARTS,), jnp.int32),
            pltpu.VMEM((2, HALF, PARTS, NT), jnp.bfloat16),
            pltpu.VMEM((PARTS, RIM * LANES), jnp.float32),
            pltpu.SemaphoreType.DMA((3,)),
            pltpu.SemaphoreType.DMA((2,)),
        ],
        compiler_params=PARAMS,
        name="pack",
    )(
        kept(fire_times),
        kept(rcv_delay),
        kept(estimate.reshape(HALF, 2, PARTS, NT)),
        kept(record),
    )
    gathered = lax.all_to_all(packed, "shot", split_axis=0, concat_axis=0, tiled=True)
    split, full = (jnp.asarray(table) for table in tables())
    updated, window = pl.pallas_call(
        main_kernel,
        out_shape=[
            jax.ShapeDtypeStruct((SHOTS, NT), jnp.bfloat16),
            jax.ShapeDtypeStruct((OWN, PARTS, NT), jnp.float32),
        ],
        in_specs=[hbm()] * 4 + [vmem()] * 3,
        out_specs=[vmem()] * 2,
        scratch_shapes=[
            pltpu.VMEM((2, SHOTS, NT), jnp.bfloat16),
            pltpu.VMEM((2 * SHOTS, NT), jnp.bfloat16),
            pltpu.VMEM((SHOTS, NT), jnp.float32),
            pltpu.VMEM((SHOTS, LANES), jnp.int32),
            pltpu.VMEM((RIM, SHOTS + 8, LANES), jnp.float32),
            pltpu.VMEM((SHOTS + 8, LANES), jnp.float32),
            pltpu.VMEM((1, FREQS), jnp.float32),
            pltpu.SMEM((OWN,), jnp.int32),
            pltpu.SMEM((PARTS,), jnp.int32),
            pltpu.VMEM((PARTS, OWN * LANES), jnp.float32),
            pltpu.SemaphoreType.DMA((4,)),
        ],
        compiler_params=PARAMS,
        name="main",
    )(
        kept(threshold.reshape(1, FREQS)),
        kept(fire_times),
        kept(rcv_delay),
        kept(record),
        gathered,
        split,
        full,
    )
    returned = lax.all_to_all(
        updated.reshape(PARTS, OWN, NT), "shot", split_axis=0, concat_axis=0, tiled=True
    )
    return pl.pallas_call(
        unpack_kernel,
        out_shape=jax.ShapeDtypeStruct((OWN, PARTS, NT), jnp.bfloat16),
        in_specs=[vmem()] * 2,
        out_specs=hbm(),
        scratch_shapes=[
            pltpu.VMEM((OWN, PARTS, NT), jnp.bfloat16),
            pltpu.SemaphoreType.DMA((4,)),
        ],
        compiler_params=PARAMS,
        name="unpack",
    )(returned, window)


def solution(mesh):
    in_specs = (P("shot", "rcv", None), P("rcv", "shot"), P("shot"), P("rcv"), P())
    out_specs = P("shot", "rcv", None)
    return jax.shard_map(shards, mesh=mesh, in_specs=in_specs, out_specs=out_specs, check_vma=False)
```

```python
import math

import jax
import jax.numpy as jnp
import ml_dtypes
import numpy as np
from jax import lax
from jax.experimental import pallas as pl
from jax.experimental.pallas import tpu as pltpu
from jax.sharding import PartitionSpec as P

SHOTS = 512
NT = 512
FREQS = 256
LANES = 128
PERIOD = 128
PARTS = 16
OWN = SHOTS // PARTS
HALF = OWN // 2
BLOCKS = NT // LANES
RIM = 6
PAYLOAD = OWN * BLOCKS + 8
CHUNKS = 2
VMEM_LIMIT = 24 << 20


def wave(rows, columns, size):
    phases = np.outer(rows, columns) % size
    angles = phases.astype(np.float64) * (2.0 * math.pi / size)
    scale = 1.0 / math.sqrt(size)
    return np.cos(angles) * scale, np.sin(angles) * scale


def rounded(table):
    return np.ascontiguousarray(table).astype(np.float32).astype(ml_dtypes.bfloat16)


def tables():
    low = np.arange(SHOTS // 2)
    even, odd = np.arange(0, SHOTS, 2), np.arange(1, SHOTS, 2)
    pieces = [np.concatenate(wave(low, part, SHOTS), axis=1) for part in (even, odd)]
    inverse = np.concatenate(wave(np.arange(SHOTS), np.arange(SHOTS), SHOTS), axis=1)
    return rounded(np.stack(pieces)), rounded(inverse)


def dot(a, b):
    return jnp.dot(a, b, preferred_element_type=jnp.float32)


def swap_table():
    row = lax.broadcasted_iota(jnp.int32, (256, 256), 0)
    column = lax.broadcasted_iota(jnp.int32, (256, 256), 1)
    source = (row & 15) * 16 + (row >> 4)
    return jnp.where(column == source, 1.0, 0.0).astype(jnp.bfloat16)


def pack_kernel(
    fire_hbm,
    delay_hbm,
    estimate_hbm,
    record_hbm,
    threshold_hbm,
    out_ref,
    own_ref,
    level_ref,
    fire_ref,
    delay_ref,
    estimate_ref,
    record_ref,
    small_sems,
    in_sems,
):
    arrivals = [
        pltpu.make_async_copy(estimate_hbm.at[:, half], estimate_ref.at[half], in_sems.at[half])
        for half in range(2)
    ]
    fires = pltpu.make_async_copy(fire_hbm, fire_ref, small_sems.at[0])
    delays = pltpu.make_async_copy(delay_hbm, delay_ref, small_sems.at[1])
    heads = pltpu.make_async_copy(
        record_hbm.at[:, pl.ds(0, RIM * LANES)], record_ref, small_sems.at[2]
    )
    arrivals[0].start()
    fires.start()
    delays.start()
    heads.start()
    arrivals[1].start()
    levels = pltpu.make_async_copy(threshold_hbm, level_ref, small_sems.at[3])
    levels.start()
    swap = swap_table()
    lane = lax.broadcasted_iota(jnp.int32, (8, LANES), 1)
    row = lax.broadcasted_iota(jnp.int32, (8, LANES), 0)
    which = lax.broadcasted_iota(jnp.int32, (PARTS, LANES), 0)
    offsets = jnp.zeros((8, LANES), jnp.int32)
    delay = jnp.zeros((PARTS, LANES), jnp.int32)
    fires.wait()
    delays.wait()
    for part in range(PARTS):
        delay = jnp.where(which == part, delay_ref[part], delay)
    for shot in range(OWN):
        jitter = fire_ref[shot] & (PERIOD - 1)
        offsets = jnp.where(lane == shot, jitter, offsets)
        own_ref[shot] = delay + jitter
    heads.wait()
    for part in range(PARTS):
        rows = (offsets + delay_ref[part]).astype(jnp.float32)
        for piece in range(RIM):
            head = record_ref[part : part + 1, piece * LANES : (piece + 1) * LANES]
            rows = jnp.where(row == piece, jnp.broadcast_to(head, (8, LANES)), rows)
        out_ref[part, BLOCKS * OWN : BLOCKS * OWN + 8, :] = rows.astype(jnp.bfloat16)
    levels.wait()
    for half in range(2):
        arrivals[half].wait()
        turned = dot(swap, estimate_ref[half].reshape(HALF * PARTS, NT)).astype(jnp.bfloat16)
        turned = turned.reshape(PARTS, HALF, NT)
        for block in range(BLOCKS):
            first = (half * BLOCKS + block) * HALF
            out_ref[:, first : first + HALF, :] = turned[:, :, block * LANES : (block + 1) * LANES]


def rotated(value, index):
    return jnp.take_along_axis(value, index, axis=1, mode="promise_in_bounds")


def read_windows(rows, offset, lane):
    near, far = lane >= offset, lane >= offset - LANES
    reach = lane + offset
    one, two = reach >= LANES, reach >= 2 * LANES
    rows = [jnp.where(near, rows[0], rows[4]), jnp.where(far, rows[1], rows[5]), *rows[2:4]]
    turned = [rotated(row, reach & (LANES - 1)) for row in rows]
    return [
        jnp.where(
            two,
            turned[(block + 2) % BLOCKS],
            jnp.where(one, turned[(block + 1) % BLOCKS], turned[block]),
        )
        for block in range(BLOCKS)
    ]


def main_kernel(
    threshold_ref,
    own_ref,
    record_ref,
    data_ref,
    split_ref,
    full_ref,
    out_ref,
    window_ref,
    stack_ref,
    shrunk_ref,
    denoised_ref,
    offset_ref,
    placed_ref,
    difference_ref,
):
    half_shots = SHOTS // 2
    data = data_ref
    lane = lax.broadcasted_iota(jnp.int32, (OWN, LANES), 1)
    row = lax.broadcasted_iota(jnp.int32, (OWN, LANES), 0)

    wide = lane[:PARTS]

    def record_window(shot):
        rows = [
            record_ref[:, piece * LANES : (piece + 1) * LANES]
            if RIM <= piece < OWN
            else jnp.zeros((PARTS, LANES), jnp.float32)
            for piece in range(shot, shot + RIM)
        ]
        for block, value in enumerate(read_windows(rows, own_ref[shot], wide)):
            window_ref[shot, :, block * LANES : (block + 1) * LANES] = 0.5 * value

    for half in range(2):
        traces = jnp.concatenate(
            [
                data[:, first : first + HALF, :].reshape(half_shots, LANES)
                for first in range(half * BLOCKS * HALF, (half + 1) * BLOCKS * HALF, HALF)
            ],
            axis=1,
        )
        real = dot(traces, full_ref[:, :FREQS]).astype(jnp.bfloat16)
        imag = (-dot(traces, full_ref[:, SHOTS : SHOTS + FREQS])).astype(jnp.bfloat16)
        stack_ref[half, :half_shots, :FREQS] = real
        stack_ref[half, :half_shots, FREQS:] = imag
        stack_ref[half, half_shots:, :FREQS] = imag
        stack_ref[half, half_shots:, FREQS:] = -real
        for shot in range(half * HALF, half * HALF + HALF):
            record_window(shot)

    waves = [dot(split_ref[half], stack_ref[half]) for half in range(2)]
    freq = lax.broadcasted_iota(jnp.int32, (1, FREQS), 1)
    weight = jnp.where(freq == 0, 1.0, 2.0).astype(jnp.float32)
    level = weight * threshold_ref[...]
    for half in range(2):
        fk = waves[0] + waves[1] if half == 0 else waves[0] - waves[1]
        real, imag = fk[:, :FREQS], fk[:, FREQS:]
        power = real * real + imag * imag + 1e-12
        factor = jnp.maximum(weight - level * lax.rsqrt(power), 0.0)
        less = (-imag * factor).astype(jnp.bfloat16)
        real = (real * factor).astype(jnp.bfloat16)
        here = slice(half * half_shots, (half + 1) * half_shots)
        there = slice(SHOTS + half * half_shots, SHOTS + (half + 1) * half_shots)
        shrunk_ref[here, :FREQS] = real
        shrunk_ref[there, :FREQS] = less
        shrunk_ref[here, FREQS:] = less
        shrunk_ref[there, FREQS:] = -real

    step = OWN

    def place(start):
        offset = offset_ref[start : start + step, :]
        index = (lane - offset) & (LANES - 1)
        near, far = lane >= offset, lane >= offset - LANES
        turned = [
            rotated(
                denoised_ref[start : start + step, block * LANES : (block + 1) * LANES], index
            )
            for block in range(BLOCKS)
        ]
        pieces = [
            jnp.where(near, turned[0], 0.0),
            jnp.where(near, turned[1], jnp.where(far, turned[0], 0.0)),
            jnp.where(near, turned[2], jnp.where(far, turned[1], turned[0])),
            jnp.where(near, turned[3], jnp.where(far, turned[2], turned[1])),
            jnp.where(near, 0.0, jnp.where(far, turned[3], turned[2])),
            jnp.where(far, 0.0, turned[3]),
        ]
        for at, piece in enumerate(pieces):
            placed_ref[at, 8 + start : 8 + start + step, :] = piece

    def subtract(start):
        total = placed_ref[0, 8 + start : 8 + start + step, :]
        for piece in range(1, RIM):
            total = total + placed_ref[piece, 8 + start - piece : 8 + start - piece + step, :]
        difference_ref[start : start + step, :] = -0.5 * total
        heads = data[start // step, BLOCKS * OWN : BLOCKS * OWN + 8, :].astype(jnp.float32)
        heads = jnp.where(row[:8] < RIM, 0.5 * heads, 0.0)
        difference_ref[start : start + 8, :] = difference_ref[start : start + 8, :] + heads

    def finish(start):
        offset = offset_ref[start : start + step, :]
        rows = [difference_ref[start + piece : start + piece + step, :] for piece in range(RIM)]
        for block, value in enumerate(read_windows(rows, offset, lane)):
            lanes = slice(block * LANES, (block + 1) * LANES)
            out_ref[start : start + step, lanes] = (
                denoised_ref[start : start + step, lanes] + value
            ).astype(jnp.bfloat16)

    for part in range(PARTS):
        rows = data[part, BLOCKS * OWN : BLOCKS * OWN + 8, :].astype(jnp.float32)
        rows = jnp.broadcast_to(rows[RIM + 1 :, :].astype(jnp.int32), (OWN, LANES))
        offset_ref[part * OWN : (part + 1) * OWN, :] = rotated(rows, row)

    inverse = jnp.concatenate([full_ref[:FREQS, :SHOTS], full_ref[:FREQS, SHOTS:]], axis=0)
    part_shots = SHOTS // CHUNKS
    steps = SHOTS // step
    subtracted, finished = 1, 1
    for part in range(CHUNKS):
        shots = slice(part * part_shots, (part + 1) * part_shots)
        back = dot(full_ref[shots, :], shrunk_ref[...]).astype(jnp.bfloat16)
        denoised_ref[shots, :] = dot(back, inverse)
        for start in range(part * part_shots, (part + 1) * part_shots, step):
            place(start)
        ready = (part + 1) * steps // CHUNKS
        for at in range(subtracted, ready):
            subtract(at * step)
        subtracted = ready
        for at in range(finished, ready - 1):
            finish(at * step)
        finished = ready - 1
    for piece in range(1, RIM):
        placed_ref[piece, 0:8, :] = placed_ref[piece, SHOTS : SHOTS + 8, :]
    subtract(0)
    difference_ref[SHOTS : SHOTS + 8, :] = difference_ref[0:8, :]
    finish(SHOTS - step)
    finish(0)


def unpack_kernel(data_ref, window_ref, out_hbm, out_ref, sems):
    swap = swap_table()
    width = NT // 2
    copies = []
    for half in range(2):
        shots = slice(half * HALF, (half + 1) * HALF)
        for side in range(2):
            lanes = slice(side * width, (side + 1) * width)
            rows = data_ref[:, shots, lanes].reshape(PARTS * HALF, width)
            out_ref[shots, :, lanes] = (
                dot(swap, rows).reshape(HALF, PARTS, width) + window_ref[shots, :, lanes]
            ).astype(jnp.bfloat16)
            place = (pl.ds(half * HALF, HALF), slice(None), pl.ds(side * width, width))
            copies.append(
                pltpu.make_async_copy(
                    out_ref.at[place], out_hbm.at[place], sems.at[2 * half + side]
                )
            )
            copies[-1].start()
    for copy in copies:
        copy.wait()


def vmem():
    return pl.BlockSpec(memory_space=pltpu.VMEM)


def hbm():
    return pl.BlockSpec(memory_space=pltpu.HBM)


def kept(value):
    return pltpu.with_memory_space_constraint(value, pltpu.HBM)


PARAMS = pltpu.CompilerParams(vmem_limit_bytes=VMEM_LIMIT)


def shards(estimate, record, fire_times, rcv_delay, threshold):
    packed, own, levels = pl.pallas_call(
        pack_kernel,
        out_shape=[
            jax.ShapeDtypeStruct((PARTS, PAYLOAD, LANES), jnp.bfloat16),
            jax.ShapeDtypeStruct((OWN, PARTS, LANES), jnp.int32),
            jax.ShapeDtypeStruct((1, FREQS), jnp.float32),
        ],
        in_specs=[hbm()] * 5,
        out_specs=[vmem()] * 3,
        scratch_shapes=[
            pltpu.SMEM((OWN,), jnp.int32),
            pltpu.SMEM((PARTS,), jnp.int32),
            pltpu.VMEM((2, HALF, PARTS, NT), jnp.bfloat16),
            pltpu.VMEM((PARTS, RIM * LANES), jnp.float32),
            pltpu.SemaphoreType.DMA((4,)),
            pltpu.SemaphoreType.DMA((2,)),
        ],
        compiler_params=PARAMS,
        name="pack",
    )(
        kept(fire_times),
        kept(rcv_delay),
        kept(estimate.reshape(HALF, 2, PARTS, NT)),
        kept(record),
        kept(threshold.reshape(1, FREQS)),
    )
    gathered = lax.all_to_all(packed, "shot", split_axis=0, concat_axis=0, tiled=True)
    split, full = (jnp.asarray(table) for table in tables())
    updated, window = pl.pallas_call(
        main_kernel,
        out_shape=[
            jax.ShapeDtypeStruct((SHOTS, NT), jnp.bfloat16),
            jax.ShapeDtypeStruct((OWN, PARTS, NT), jnp.float32),
        ],
        in_specs=[vmem()] * 6,
        out_specs=[vmem()] * 2,
        scratch_shapes=[
            pltpu.VMEM((2, SHOTS, NT), jnp.bfloat16),
            pltpu.VMEM((2 * SHOTS, NT), jnp.bfloat16),
            pltpu.VMEM((SHOTS, NT), jnp.float32),
            pltpu.VMEM((SHOTS, LANES), jnp.int32),
            pltpu.VMEM((RIM, SHOTS + 8, LANES), jnp.float32),
            pltpu.VMEM((SHOTS + 8, LANES), jnp.float32),
        ],
        compiler_params=PARAMS,
        name="main",
    )(
        levels,
        own,
        record,
        gathered,
        split,
        full,
    )
    returned = lax.all_to_all(
        updated.reshape(PARTS, OWN, NT), "shot", split_axis=0, concat_axis=0, tiled=True
    )
    return pl.pallas_call(
        unpack_kernel,
        out_shape=jax.ShapeDtypeStruct((OWN, PARTS, NT), jnp.bfloat16),
        in_specs=[vmem()] * 2,
        out_specs=hbm(),
        scratch_shapes=[
            pltpu.VMEM((OWN, PARTS, NT), jnp.bfloat16),
            pltpu.SemaphoreType.DMA((4,)),
        ],
        compiler_params=PARAMS,
        name="unpack",
    )(returned, window)


def solution(mesh):
    in_specs = (P("shot", "rcv", None), P("rcv", "shot"), P("shot"), P("rcv"), P())
    out_specs = P("shot", "rcv", None)
    return jax.shard_map(shards, mesh=mesh, in_specs=in_specs, out_specs=out_specs, check_vma=False)
```

```python
import math

import jax
import jax.numpy as jnp
import ml_dtypes
import numpy as np
from jax import lax
from jax.experimental import pallas as pl
from jax.experimental.pallas import tpu as pltpu
from jax.sharding import PartitionSpec as P

SHOTS = 512
NT = 512
FREQS = 256
LANES = 128
PERIOD = 128
PARTS = 16
OWN = SHOTS // PARTS
HALF = OWN // 2
BLOCKS = NT // LANES
RIM = 6
PAYLOAD = OWN * BLOCKS + 8
CHUNKS = 2
VMEM_LIMIT = 24 << 20


def wave(rows, columns, size):
    phases = np.outer(rows, columns) % size
    angles = phases.astype(np.float64) * (2.0 * math.pi / size)
    scale = 1.0 / math.sqrt(size)
    return np.cos(angles) * scale, np.sin(angles) * scale


def rounded(table):
    return np.ascontiguousarray(table).astype(np.float32).astype(ml_dtypes.bfloat16)


def tables():
    low = np.arange(SHOTS // 2)
    even, odd = np.arange(0, SHOTS, 2), np.arange(1, SHOTS, 2)
    pieces = [np.concatenate(wave(low, part, SHOTS), axis=1) for part in (even, odd)]
    inverse = np.concatenate(wave(np.arange(SHOTS), np.arange(SHOTS), SHOTS), axis=1)
    return rounded(np.stack(pieces)), rounded(inverse)


def dot(a, b):
    return jnp.dot(a, b, preferred_element_type=jnp.float32)


def pack_kernel(
    fire_hbm,
    delay_hbm,
    estimate_hbm,
    record_hbm,
    threshold_hbm,
    out_ref,
    own_ref,
    level_ref,
    fire_ref,
    delay_ref,
    estimate_ref,
    record_ref,
    small_sems,
    in_sems,
):
    arrivals = [
        pltpu.make_async_copy(estimate_hbm.at[:, half], estimate_ref.at[half], in_sems.at[half])
        for half in range(2)
    ]
    fires = pltpu.make_async_copy(fire_hbm, fire_ref, small_sems.at[0])
    delays = pltpu.make_async_copy(delay_hbm, delay_ref, small_sems.at[1])
    heads = pltpu.make_async_copy(
        record_hbm.at[:, pl.ds(0, RIM * LANES)], record_ref, small_sems.at[2]
    )
    arrivals[0].start()
    arrivals[1].start()
    fires.start()
    delays.start()
    heads.start()
    levels = pltpu.make_async_copy(threshold_hbm, level_ref, small_sems.at[3])
    levels.start()
    lane = lax.broadcasted_iota(jnp.int32, (8, LANES), 1)
    row = lax.broadcasted_iota(jnp.int32, (8, LANES), 0)
    which = lax.broadcasted_iota(jnp.int32, (PARTS, LANES), 0)
    offsets = jnp.zeros((8, LANES), jnp.int32)
    delay = jnp.zeros((PARTS, LANES), jnp.int32)
    fires.wait()
    delays.wait()
    for part in range(PARTS):
        delay = jnp.where(which == part, delay_ref[part], delay)
    for shot in range(OWN):
        jitter = fire_ref[shot] & (PERIOD - 1)
        offsets = jnp.where(lane == shot, jitter, offsets)
        own_ref[shot] = delay + jitter
    heads.wait()
    for part in range(PARTS):
        rows = (offsets + delay_ref[part]).astype(jnp.float32)
        for piece in range(RIM):
            head = record_ref[part : part + 1, piece * LANES : (piece + 1) * LANES]
            rows = jnp.where(row == piece, jnp.broadcast_to(head, (8, LANES)), rows)
        out_ref[part, BLOCKS * OWN : BLOCKS * OWN + 8, :] = rows.astype(jnp.bfloat16)
    levels.wait()
    for half in range(2):
        arrivals[half].wait()
        turned = jnp.swapaxes(estimate_ref[half], 0, 1)
        for block in range(BLOCKS):
            first = (half * BLOCKS + block) * HALF
            out_ref[:, first : first + HALF, :] = turned[:, :, block * LANES : (block + 1) * LANES]


def rotated(value, index):
    return jnp.take_along_axis(value, index, axis=1, mode="promise_in_bounds")


def read_windows(rows, offset, lane):
    near, far = lane >= offset, lane >= offset - LANES
    reach = lane + offset
    one, two = reach >= LANES, reach >= 2 * LANES
    rows = [jnp.where(near, rows[0], rows[4]), jnp.where(far, rows[1], rows[5]), *rows[2:4]]
    turned = [rotated(row, reach & (LANES - 1)) for row in rows]
    return [
        jnp.where(
            two,
            turned[(block + 2) % BLOCKS],
            jnp.where(one, turned[(block + 1) % BLOCKS], turned[block]),
        )
        for block in range(BLOCKS)
    ]


def main_kernel(
    threshold_ref,
    own_ref,
    record_ref,
    data_ref,
    split_ref,
    full_ref,
    out_ref,
    window_ref,
    stack_ref,
    shrunk_ref,
    denoised_ref,
    offset_ref,
    placed_ref,
    difference_ref,
):
    half_shots = SHOTS // 2
    data = data_ref
    lane = lax.broadcasted_iota(jnp.int32, (OWN, LANES), 1)
    row = lax.broadcasted_iota(jnp.int32, (OWN, LANES), 0)

    wide = lane[:PARTS]

    def record_window(shot):
        rows = [
            record_ref[:, piece * LANES : (piece + 1) * LANES]
            if RIM <= piece < OWN
            else jnp.zeros((PARTS, LANES), jnp.float32)
            for piece in range(shot, shot + RIM)
        ]
        for block, value in enumerate(read_windows(rows, own_ref[shot], wide)):
            window_ref[shot, :, block * LANES : (block + 1) * LANES] = 0.5 * value

    for half in range(2):
        traces = jnp.concatenate(
            [
                data[:, first : first + HALF, :].reshape(half_shots, LANES)
                for first in range(half * BLOCKS * HALF, (half + 1) * BLOCKS * HALF, HALF)
            ],
            axis=1,
        )
        real = dot(traces, full_ref[:, :FREQS]).astype(jnp.bfloat16)
        imag = (-dot(traces, full_ref[:, SHOTS : SHOTS + FREQS])).astype(jnp.bfloat16)
        stack_ref[half, :half_shots, :FREQS] = real
        stack_ref[half, :half_shots, FREQS:] = imag
        stack_ref[half, half_shots:, :FREQS] = imag
        stack_ref[half, half_shots:, FREQS:] = -real
        for shot in range(half * HALF, half * HALF + HALF):
            record_window(shot)

    waves = [dot(split_ref[half], stack_ref[half]) for half in range(2)]
    freq = lax.broadcasted_iota(jnp.int32, (1, FREQS), 1)
    weight = jnp.where(freq == 0, 1.0, 2.0).astype(jnp.float32)
    level = weight * threshold_ref[...]
    for half in range(2):
        fk = waves[0] + waves[1] if half == 0 else waves[0] - waves[1]
        real, imag = fk[:, :FREQS], fk[:, FREQS:]
        power = real * real + imag * imag + 1e-12
        factor = jnp.maximum(weight - level * lax.rsqrt(power), 0.0)
        less = (-imag * factor).astype(jnp.bfloat16)
        real = (real * factor).astype(jnp.bfloat16)
        here = slice(half * half_shots, (half + 1) * half_shots)
        there = slice(SHOTS + half * half_shots, SHOTS + (half + 1) * half_shots)
        shrunk_ref[here, :FREQS] = real
        shrunk_ref[there, :FREQS] = less
        shrunk_ref[here, FREQS:] = less
        shrunk_ref[there, FREQS:] = -real

    step = OWN

    def place(start):
        offset = offset_ref[start : start + step, :]
        index = (lane - offset) & (LANES - 1)
        near, far = lane >= offset, lane >= offset - LANES
        turned = [
            rotated(
                denoised_ref[start : start + step, block * LANES : (block + 1) * LANES], index
            )
            for block in range(BLOCKS)
        ]
        pieces = [
            jnp.where(near, turned[0], 0.0),
            jnp.where(near, turned[1], jnp.where(far, turned[0], 0.0)),
            jnp.where(near, turned[2], jnp.where(far, turned[1], turned[0])),
            jnp.where(near, turned[3], jnp.where(far, turned[2], turned[1])),
            jnp.where(near, 0.0, jnp.where(far, turned[3], turned[2])),
            jnp.where(far, 0.0, turned[3]),
        ]
        for at, piece in enumerate(pieces):
            placed_ref[at, 8 + start : 8 + start + step, :] = piece

    def subtract(start):
        total = placed_ref[0, 8 + start : 8 + start + step, :]
        for piece in range(1, RIM):
            total = total + placed_ref[piece, 8 + start - piece : 8 + start - piece + step, :]
        difference_ref[start : start + step, :] = -0.5 * total
        heads = data[start // step, BLOCKS * OWN : BLOCKS * OWN + 8, :].astype(jnp.float32)
        heads = jnp.where(row[:8] < RIM, 0.5 * heads, 0.0)
        difference_ref[start : start + 8, :] = difference_ref[start : start + 8, :] + heads

    def finish(start):
        offset = offset_ref[start : start + step, :]
        rows = [difference_ref[start + piece : start + piece + step, :] for piece in range(RIM)]
        for block, value in enumerate(read_windows(rows, offset, lane)):
            lanes = slice(block * LANES, (block + 1) * LANES)
            out_ref[start : start + step, lanes] = (
                denoised_ref[start : start + step, lanes] + value
            ).astype(jnp.bfloat16)

    for part in range(PARTS):
        rows = data[part, BLOCKS * OWN : BLOCKS * OWN + 8, :].astype(jnp.float32)
        rows = jnp.broadcast_to(rows[RIM + 1 :, :].astype(jnp.int32), (OWN, LANES))
        offset_ref[part * OWN : (part + 1) * OWN, :] = rotated(rows, row)

    inverse = jnp.concatenate([full_ref[:FREQS, :SHOTS], full_ref[:FREQS, SHOTS:]], axis=0)
    part_shots = SHOTS // CHUNKS
    steps = SHOTS // step
    subtracted, finished = 1, 1
    for part in range(CHUNKS):
        shots = slice(part * part_shots, (part + 1) * part_shots)
        back = dot(full_ref[shots, :], shrunk_ref[...]).astype(jnp.bfloat16)
        denoised_ref[shots, :] = dot(back, inverse)
        for start in range(part * part_shots, (part + 1) * part_shots, step):
            place(start)
        ready = (part + 1) * steps // CHUNKS
        for at in range(subtracted, ready):
            subtract(at * step)
        subtracted = ready
        for at in range(finished, ready - 1):
            finish(at * step)
        finished = ready - 1
    for piece in range(1, RIM):
        placed_ref[piece, 0:8, :] = placed_ref[piece, SHOTS : SHOTS + 8, :]
    subtract(0)
    difference_ref[SHOTS : SHOTS + 8, :] = difference_ref[0:8, :]
    finish(SHOTS - step)
    finish(0)


def unpack_kernel(data_ref, window_ref, out_hbm, out_ref, sems):
    width = NT // 2
    copies = []
    for half in range(2):
        shots = slice(half * HALF, (half + 1) * HALF)
        for side in range(2):
            lanes = slice(side * width, (side + 1) * width)
            rows = data_ref[:, shots, lanes]
            out_ref[shots, :, lanes] = (
                jnp.swapaxes(rows, 0, 1).astype(jnp.float32) + window_ref[shots, :, lanes]
            ).astype(jnp.bfloat16)
            place = (pl.ds(half * HALF, HALF), slice(None), pl.ds(side * width, width))
            copies.append(
                pltpu.make_async_copy(
                    out_ref.at[place], out_hbm.at[place], sems.at[2 * half + side]
                )
            )
            copies[-1].start()
    for copy in copies:
        copy.wait()


def vmem():
    return pl.BlockSpec(memory_space=pltpu.VMEM)


def hbm():
    return pl.BlockSpec(memory_space=pltpu.HBM)


def kept(value):
    return pltpu.with_memory_space_constraint(value, pltpu.HBM)


PARAMS = pltpu.CompilerParams(vmem_limit_bytes=VMEM_LIMIT)


def shards(estimate, record, fire_times, rcv_delay, threshold):
    packed, own, levels = pl.pallas_call(
        pack_kernel,
        out_shape=[
            jax.ShapeDtypeStruct((PARTS, PAYLOAD, LANES), jnp.bfloat16),
            jax.ShapeDtypeStruct((OWN, PARTS, LANES), jnp.int32),
            jax.ShapeDtypeStruct((1, FREQS), jnp.float32),
        ],
        in_specs=[hbm()] * 5,
        out_specs=[vmem()] * 3,
        scratch_shapes=[
            pltpu.SMEM((OWN,), jnp.int32),
            pltpu.SMEM((PARTS,), jnp.int32),
            pltpu.VMEM((2, HALF, PARTS, NT), jnp.bfloat16),
            pltpu.VMEM((PARTS, RIM * LANES), jnp.float32),
            pltpu.SemaphoreType.DMA((4,)),
            pltpu.SemaphoreType.DMA((2,)),
        ],
        compiler_params=PARAMS,
        name="pack",
    )(
        kept(fire_times),
        kept(rcv_delay),
        kept(estimate.reshape(HALF, 2, PARTS, NT)),
        kept(record),
        kept(threshold.reshape(1, FREQS)),
    )
    gathered = lax.all_to_all(packed, "shot", split_axis=0, concat_axis=0, tiled=True)
    split, full = (jnp.asarray(table) for table in tables())
    updated, window = pl.pallas_call(
        main_kernel,
        out_shape=[
            jax.ShapeDtypeStruct((SHOTS, NT), jnp.bfloat16),
            jax.ShapeDtypeStruct((OWN, PARTS, NT), jnp.float32),
        ],
        in_specs=[vmem()] * 6,
        out_specs=[vmem()] * 2,
        scratch_shapes=[
            pltpu.VMEM((2, SHOTS, NT), jnp.bfloat16),
            pltpu.VMEM((2 * SHOTS, NT), jnp.bfloat16),
            pltpu.VMEM((SHOTS, NT), jnp.float32),
            pltpu.VMEM((SHOTS, LANES), jnp.int32),
            pltpu.VMEM((RIM, SHOTS + 8, LANES), jnp.float32),
            pltpu.VMEM((SHOTS + 8, LANES), jnp.float32),
        ],
        compiler_params=PARAMS,
        name="main",
    )(
        levels,
        own,
        record,
        gathered,
        split,
        full,
    )
    returned = lax.all_to_all(
        updated.reshape(PARTS, OWN, NT), "shot", split_axis=0, concat_axis=0, tiled=True
    )
    return pl.pallas_call(
        unpack_kernel,
        out_shape=jax.ShapeDtypeStruct((OWN, PARTS, NT), jnp.bfloat16),
        in_specs=[vmem()] * 2,
        out_specs=hbm(),
        scratch_shapes=[
            pltpu.VMEM((OWN, PARTS, NT), jnp.bfloat16),
            pltpu.SemaphoreType.DMA((4,)),
        ],
        compiler_params=PARAMS,
        name="unpack",
    )(returned, window)


def solution(mesh):
    in_specs = (P("shot", "rcv", None), P("rcv", "shot"), P("shot"), P("rcv"), P())
    out_specs = P("shot", "rcv", None)
    return jax.shard_map(shards, mesh=mesh, in_specs=in_specs, out_specs=out_specs, check_vma=False)
```

```python
import math

import jax
import jax.numpy as jnp
import ml_dtypes
import numpy as np
from jax import lax
from jax.experimental import pallas as pl
from jax.experimental.pallas import tpu as pltpu
from jax.sharding import PartitionSpec as P

SHOTS = 512
NT = 512
FREQS = 256
LANES = 128
PERIOD = 128
PARTS = 16
OWN = SHOTS // PARTS
HALF = OWN // 2
BLOCKS = NT // LANES
RIM = 6
PAYLOAD = OWN * BLOCKS + 8
CHUNKS = 2
VMEM_LIMIT = 24 << 20


def wave(rows, columns, size):
    phases = np.outer(rows, columns) % size
    angles = phases.astype(np.float64) * (2.0 * math.pi / size)
    scale = 1.0 / math.sqrt(size)
    return np.cos(angles) * scale, np.sin(angles) * scale


def rounded(table):
    return np.ascontiguousarray(table).astype(np.float32).astype(ml_dtypes.bfloat16)


def tables():
    low = np.arange(SHOTS // 2)
    even, odd = np.arange(0, SHOTS, 2), np.arange(1, SHOTS, 2)
    pieces = [np.concatenate(wave(low, part, SHOTS), axis=1) for part in (even, odd)]
    inverse = np.concatenate(wave(np.arange(SHOTS), np.arange(SHOTS), SHOTS), axis=1)
    return rounded(np.stack(pieces)), rounded(inverse)


def dot(a, b):
    return jnp.dot(a, b, preferred_element_type=jnp.float32)


def pack_kernel(
    fire_hbm,
    delay_hbm,
    estimate_hbm,
    record_hbm,
    threshold_hbm,
    out_ref,
    own_ref,
    level_ref,
    fire_ref,
    delay_ref,
    estimate_ref,
    record_ref,
    small_sems,
    in_sems,
):
    arrivals = [
        pltpu.make_async_copy(estimate_hbm.at[:, half], estimate_ref.at[half], in_sems.at[half])
        for half in range(2)
    ]
    fires = pltpu.make_async_copy(fire_hbm, fire_ref, small_sems.at[0])
    delays = pltpu.make_async_copy(delay_hbm, delay_ref, small_sems.at[1])
    heads = pltpu.make_async_copy(
        record_hbm.at[:, pl.ds(0, RIM * LANES)], record_ref, small_sems.at[2]
    )
    arrivals[0].start()
    arrivals[1].start()
    fires.start()
    delays.start()
    heads.start()
    levels = pltpu.make_async_copy(threshold_hbm, level_ref, small_sems.at[3])
    levels.start()
    lane = lax.broadcasted_iota(jnp.int32, (8, LANES), 1)
    row = lax.broadcasted_iota(jnp.int32, (8, LANES), 0)
    which = lax.broadcasted_iota(jnp.int32, (PARTS, LANES), 0)
    offsets = jnp.zeros((8, LANES), jnp.int32)
    delay = jnp.zeros((PARTS, LANES), jnp.int32)
    fires.wait()
    delays.wait()
    for part in range(PARTS):
        delay = jnp.where(which == part, delay_ref[part], delay)
    for shot in range(OWN):
        jitter = fire_ref[shot] & (PERIOD - 1)
        offsets = jnp.where(lane == shot, jitter, offsets)
        own_ref[shot] = delay + jitter
    def turn(half):
        arrivals[half].wait()
        turned = jnp.swapaxes(estimate_ref[half], 0, 1)
        for block in range(BLOCKS):
            first = (half * BLOCKS + block) * HALF
            out_ref[:, first : first + HALF, :] = turned[:, :, block * LANES : (block + 1) * LANES]

    turn(0)
    heads.wait()
    for part in range(PARTS):
        rows = (offsets + delay_ref[part]).astype(jnp.float32)
        for piece in range(RIM):
            head = record_ref[part : part + 1, piece * LANES : (piece + 1) * LANES]
            rows = jnp.where(row == piece, jnp.broadcast_to(head, (8, LANES)), rows)
        out_ref[part, BLOCKS * OWN : BLOCKS * OWN + 8, :] = rows.astype(jnp.bfloat16)
    turn(1)
    levels.wait()


def rotated(value, index):
    return jnp.take_along_axis(value, index, axis=1, mode="promise_in_bounds")


def read_windows(rows, offset, lane):
    near, far = lane >= offset, lane >= offset - LANES
    reach = lane + offset
    one, two = reach >= LANES, reach >= 2 * LANES
    rows = [jnp.where(near, rows[0], rows[4]), jnp.where(far, rows[1], rows[5]), *rows[2:4]]
    turned = [rotated(row, reach & (LANES - 1)) for row in rows]
    return [
        jnp.where(
            two,
            turned[(block + 2) % BLOCKS],
            jnp.where(one, turned[(block + 1) % BLOCKS], turned[block]),
        )
        for block in range(BLOCKS)
    ]


def main_kernel(
    threshold_ref,
    own_ref,
    record_ref,
    data_ref,
    split_ref,
    full_ref,
    out_ref,
    window_ref,
    stack_ref,
    shrunk_ref,
    denoised_ref,
    offset_ref,
    placed_ref,
    difference_ref,
):
    half_shots = SHOTS // 2
    data = data_ref
    lane = lax.broadcasted_iota(jnp.int32, (OWN, LANES), 1)
    row = lax.broadcasted_iota(jnp.int32, (OWN, LANES), 0)

    wide = lane[:PARTS]

    def record_window(shot):
        rows = [
            record_ref[:, piece * LANES : (piece + 1) * LANES]
            if RIM <= piece < OWN
            else jnp.zeros((PARTS, LANES), jnp.float32)
            for piece in range(shot, shot + RIM)
        ]
        for block, value in enumerate(read_windows(rows, own_ref[shot], wide)):
            window_ref[shot, :, block * LANES : (block + 1) * LANES] = 0.5 * value

    for half in range(2):
        traces = jnp.concatenate(
            [
                data[:, first : first + HALF, :].reshape(half_shots, LANES)
                for first in range(half * BLOCKS * HALF, (half + 1) * BLOCKS * HALF, HALF)
            ],
            axis=1,
        )
        real = dot(traces, full_ref[:, :FREQS]).astype(jnp.bfloat16)
        imag = (-dot(traces, full_ref[:, SHOTS : SHOTS + FREQS])).astype(jnp.bfloat16)
        stack_ref[half, :half_shots, :FREQS] = real
        stack_ref[half, :half_shots, FREQS:] = imag
        stack_ref[half, half_shots:, :FREQS] = imag
        stack_ref[half, half_shots:, FREQS:] = -real
        for shot in range(half * HALF, half * HALF + HALF):
            record_window(shot)

    waves = [dot(split_ref[half], stack_ref[half]) for half in range(2)]
    freq = lax.broadcasted_iota(jnp.int32, (1, FREQS), 1)
    weight = jnp.where(freq == 0, 1.0, 2.0).astype(jnp.float32)
    level = weight * threshold_ref[...]
    for half in range(2):
        fk = waves[0] + waves[1] if half == 0 else waves[0] - waves[1]
        real, imag = fk[:, :FREQS], fk[:, FREQS:]
        power = real * real + imag * imag + 1e-12
        factor = jnp.maximum(weight - level * lax.rsqrt(power), 0.0)
        less = (-imag * factor).astype(jnp.bfloat16)
        real = (real * factor).astype(jnp.bfloat16)
        here = slice(half * half_shots, (half + 1) * half_shots)
        there = slice(SHOTS + half * half_shots, SHOTS + (half + 1) * half_shots)
        shrunk_ref[here, :FREQS] = real
        shrunk_ref[there, :FREQS] = less
        shrunk_ref[here, FREQS:] = less
        shrunk_ref[there, FREQS:] = -real

    step = OWN

    def place(start):
        offset = offset_ref[start : start + step, :]
        index = (lane - offset) & (LANES - 1)
        near, far = lane >= offset, lane >= offset - LANES
        turned = [
            rotated(
                denoised_ref[start : start + step, block * LANES : (block + 1) * LANES], index
            )
            for block in range(BLOCKS)
        ]
        pieces = [
            jnp.where(near, turned[0], 0.0),
            jnp.where(near, turned[1], jnp.where(far, turned[0], 0.0)),
            jnp.where(near, turned[2], jnp.where(far, turned[1], turned[0])),
            jnp.where(near, turned[3], jnp.where(far, turned[2], turned[1])),
            jnp.where(near, 0.0, jnp.where(far, turned[3], turned[2])),
            jnp.where(far, 0.0, turned[3]),
        ]
        for at, piece in enumerate(pieces):
            placed_ref[at, 8 + start : 8 + start + step, :] = piece

    def subtract(start):
        total = placed_ref[0, 8 + start : 8 + start + step, :]
        for piece in range(1, RIM):
            total = total + placed_ref[piece, 8 + start - piece : 8 + start - piece + step, :]
        difference_ref[start : start + step, :] = -0.5 * total
        heads = data[start // step, BLOCKS * OWN : BLOCKS * OWN + 8, :].astype(jnp.float32)
        heads = jnp.where(row[:8] < RIM, 0.5 * heads, 0.0)
        difference_ref[start : start + 8, :] = difference_ref[start : start + 8, :] + heads

    def finish(start):
        offset = offset_ref[start : start + step, :]
        rows = [difference_ref[start + piece : start + piece + step, :] for piece in range(RIM)]
        for block, value in enumerate(read_windows(rows, offset, lane)):
            lanes = slice(block * LANES, (block + 1) * LANES)
            out_ref[start : start + step, lanes] = (
                denoised_ref[start : start + step, lanes] + value
            ).astype(jnp.bfloat16)

    for part in range(PARTS):
        rows = data[part, BLOCKS * OWN : BLOCKS * OWN + 8, :].astype(jnp.float32)
        rows = jnp.broadcast_to(rows[RIM + 1 :, :].astype(jnp.int32), (OWN, LANES))
        offset_ref[part * OWN : (part + 1) * OWN, :] = rotated(rows, row)

    inverse = jnp.concatenate([full_ref[:FREQS, :SHOTS], full_ref[:FREQS, SHOTS:]], axis=0)
    part_shots = SHOTS // CHUNKS
    steps = SHOTS // step
    subtracted, finished = 1, 1
    for part in range(CHUNKS):
        shots = slice(part * part_shots, (part + 1) * part_shots)
        back = dot(full_ref[shots, :], shrunk_ref[...]).astype(jnp.bfloat16)
        denoised_ref[shots, :] = dot(back, inverse)
        for start in range(part * part_shots, (part + 1) * part_shots, step):
            place(start)
        ready = (part + 1) * steps // CHUNKS
        for at in range(subtracted, ready):
            subtract(at * step)
        subtracted = ready
        for at in range(finished, ready - 1):
            finish(at * step)
        finished = ready - 1
    for piece in range(1, RIM):
        placed_ref[piece, 0:8, :] = placed_ref[piece, SHOTS : SHOTS + 8, :]
    subtract(0)
    difference_ref[SHOTS : SHOTS + 8, :] = difference_ref[0:8, :]
    finish(SHOTS - step)
    finish(0)


def unpack_kernel(data_ref, window_ref, out_hbm, out_ref, sems):
    width = NT // 2
    copies = []
    for half in range(2):
        shots = slice(half * HALF, (half + 1) * HALF)
        for side in range(2):
            lanes = slice(side * width, (side + 1) * width)
            rows = data_ref[:, shots, lanes]
            out_ref[shots, :, lanes] = (
                jnp.swapaxes(rows, 0, 1).astype(jnp.float32) + window_ref[shots, :, lanes]
            ).astype(jnp.bfloat16)
            place = (pl.ds(half * HALF, HALF), slice(None), pl.ds(side * width, width))
            copies.append(
                pltpu.make_async_copy(
                    out_ref.at[place], out_hbm.at[place], sems.at[2 * half + side]
                )
            )
            copies[-1].start()
    for copy in copies:
        copy.wait()


def vmem():
    return pl.BlockSpec(memory_space=pltpu.VMEM)


def hbm():
    return pl.BlockSpec(memory_space=pltpu.HBM)


def kept(value):
    return pltpu.with_memory_space_constraint(value, pltpu.HBM)


PARAMS = pltpu.CompilerParams(vmem_limit_bytes=VMEM_LIMIT)


def shards(estimate, record, fire_times, rcv_delay, threshold):
    packed, own, levels = pl.pallas_call(
        pack_kernel,
        out_shape=[
            jax.ShapeDtypeStruct((PARTS, PAYLOAD, LANES), jnp.bfloat16),
            jax.ShapeDtypeStruct((OWN, PARTS, LANES), jnp.int32),
            jax.ShapeDtypeStruct((1, FREQS), jnp.float32),
        ],
        in_specs=[hbm()] * 5,
        out_specs=[vmem()] * 3,
        scratch_shapes=[
            pltpu.SMEM((OWN,), jnp.int32),
            pltpu.SMEM((PARTS,), jnp.int32),
            pltpu.VMEM((2, HALF, PARTS, NT), jnp.bfloat16),
            pltpu.VMEM((PARTS, RIM * LANES), jnp.float32),
            pltpu.SemaphoreType.DMA((4,)),
            pltpu.SemaphoreType.DMA((2,)),
        ],
        compiler_params=PARAMS,
        name="pack",
    )(
        kept(fire_times),
        kept(rcv_delay),
        kept(estimate.reshape(HALF, 2, PARTS, NT)),
        kept(record),
        kept(threshold.reshape(1, FREQS)),
    )
    gathered = lax.all_to_all(packed, "shot", split_axis=0, concat_axis=0, tiled=True)
    split, full = (jnp.asarray(table) for table in tables())
    updated, window = pl.pallas_call(
        main_kernel,
        out_shape=[
            jax.ShapeDtypeStruct((SHOTS, NT), jnp.bfloat16),
            jax.ShapeDtypeStruct((OWN, PARTS, NT), jnp.float32),
        ],
        in_specs=[vmem()] * 6,
        out_specs=[vmem()] * 2,
        scratch_shapes=[
            pltpu.VMEM((2, SHOTS, NT), jnp.bfloat16),
            pltpu.VMEM((2 * SHOTS, NT), jnp.bfloat16),
            pltpu.VMEM((SHOTS, NT), jnp.float32),
            pltpu.VMEM((SHOTS, LANES), jnp.int32),
            pltpu.VMEM((RIM, SHOTS + 8, LANES), jnp.float32),
            pltpu.VMEM((SHOTS + 8, LANES), jnp.float32),
        ],
        compiler_params=PARAMS,
        name="main",
    )(
        levels,
        own,
        record,
        gathered,
        split,
        full,
    )
    returned = lax.all_to_all(
        updated.reshape(PARTS, OWN, NT), "shot", split_axis=0, concat_axis=0, tiled=True
    )
    return pl.pallas_call(
        unpack_kernel,
        out_shape=jax.ShapeDtypeStruct((OWN, PARTS, NT), jnp.bfloat16),
        in_specs=[vmem()] * 2,
        out_specs=hbm(),
        scratch_shapes=[
            pltpu.VMEM((OWN, PARTS, NT), jnp.bfloat16),
            pltpu.SemaphoreType.DMA((4,)),
        ],
        compiler_params=PARAMS,
        name="unpack",
    )(returned, window)


def solution(mesh):
    in_specs = (P("shot", "rcv", None), P("rcv", "shot"), P("shot"), P("rcv"), P())
    out_specs = P("shot", "rcv", None)
    return jax.shard_map(shards, mesh=mesh, in_specs=in_specs, out_specs=out_specs, check_vma=False)
```

```python
import math

import jax
import jax.numpy as jnp
import ml_dtypes
import numpy as np
from jax import lax
from jax.experimental import pallas as pl
from jax.experimental.pallas import tpu as pltpu
from jax.sharding import PartitionSpec as P

SHOTS = 512
NT = 512
FREQS = 256
LANES = 128
PERIOD = 128
PARTS = 16
OWN = SHOTS // PARTS
HALF = OWN // 2
BLOCKS = NT // LANES
RIM = 6
PAYLOAD = OWN * BLOCKS + 8
CHUNKS = 2
VMEM_LIMIT = 24 << 20


def wave(rows, columns, size):
    phases = np.outer(rows, columns) % size
    angles = phases.astype(np.float64) * (2.0 * math.pi / size)
    scale = 1.0 / math.sqrt(size)
    return np.cos(angles) * scale, np.sin(angles) * scale


def rounded(table):
    return np.ascontiguousarray(table).astype(np.float32).astype(ml_dtypes.bfloat16)


def tables():
    low = np.arange(SHOTS // 2)
    even, odd = np.arange(0, SHOTS, 2), np.arange(1, SHOTS, 2)
    pieces = [np.concatenate(wave(low, part, SHOTS), axis=1) for part in (even, odd)]
    inverse = np.concatenate(wave(np.arange(SHOTS), np.arange(SHOTS), SHOTS), axis=1)
    return rounded(np.stack(pieces)), rounded(inverse)


def dot(a, b):
    return jnp.dot(a, b, preferred_element_type=jnp.float32)


def pack_kernel(
    fire_hbm,
    delay_hbm,
    estimate_hbm,
    record_hbm,
    threshold_hbm,
    out_ref,
    own_ref,
    level_ref,
    fire_ref,
    delay_ref,
    estimate_ref,
    record_ref,
    small_sems,
    in_sems,
):
    arrivals = [
        pltpu.make_async_copy(estimate_hbm.at[:, half], estimate_ref.at[half], in_sems.at[half])
        for half in range(2)
    ]
    fires = pltpu.make_async_copy(fire_hbm, fire_ref, small_sems.at[0])
    delays = pltpu.make_async_copy(delay_hbm, delay_ref, small_sems.at[1])
    heads = pltpu.make_async_copy(
        record_hbm.at[:, pl.ds(0, RIM * LANES)], record_ref, small_sems.at[2]
    )
    arrivals[0].start()
    arrivals[1].start()
    fires.start()
    delays.start()
    heads.start()
    levels = pltpu.make_async_copy(threshold_hbm, level_ref, small_sems.at[3])
    levels.start()
    lane = lax.broadcasted_iota(jnp.int32, (8, LANES), 1)
    row = lax.broadcasted_iota(jnp.int32, (8, LANES), 0)
    which = lax.broadcasted_iota(jnp.int32, (PARTS, LANES), 0)
    offsets = jnp.zeros((8, LANES), jnp.int32)
    delay = jnp.zeros((PARTS, LANES), jnp.int32)
    fires.wait()
    delays.wait()
    for part in range(PARTS):
        delay = jnp.where(which == part, delay_ref[part], delay)
    for shot in range(OWN):
        jitter = fire_ref[shot] & (PERIOD - 1)
        offsets = jnp.where(lane == shot, jitter, offsets)
        own_ref[shot] = delay + jitter
    heads.wait()
    for part in range(PARTS):
        rows = (offsets + delay_ref[part]).astype(jnp.float32)
        for piece in range(RIM):
            head = record_ref[part : part + 1, piece * LANES : (piece + 1) * LANES]
            rows = jnp.where(row == piece, jnp.broadcast_to(head, (8, LANES)), rows)
        out_ref[part, BLOCKS * OWN : BLOCKS * OWN + 8, :] = rows.astype(jnp.bfloat16)
    levels.wait()
    for half in range(2):
        arrivals[half].wait()
        turned = jnp.swapaxes(estimate_ref[half], 0, 1)
        for block in range(BLOCKS):
            first = (half * BLOCKS + block) * HALF
            out_ref[:, first : first + HALF, :] = turned[:, :, block * LANES : (block + 1) * LANES]


def rotated(value, index):
    return jnp.take_along_axis(value, index, axis=1, mode="promise_in_bounds")


def read_windows(rows, offset, lane):
    near, far = lane >= offset, lane >= offset - LANES
    reach = lane + offset
    one, two = reach >= LANES, reach >= 2 * LANES
    rows = [jnp.where(near, rows[0], rows[4]), jnp.where(far, rows[1], rows[5]), *rows[2:4]]
    turned = [rotated(row, reach & (LANES - 1)) for row in rows]
    return [
        jnp.where(
            two,
            turned[(block + 2) % BLOCKS],
            jnp.where(one, turned[(block + 1) % BLOCKS], turned[block]),
        )
        for block in range(BLOCKS)
    ]


def main_kernel(
    threshold_ref,
    own_ref,
    record_ref,
    data_ref,
    split_ref,
    full_ref,
    out_ref,
    window_ref,
    stack_ref,
    shrunk_ref,
    denoised_ref,
    offset_ref,
    placed_ref,
    difference_ref,
):
    half_shots = SHOTS // 2
    data = data_ref
    lane = lax.broadcasted_iota(jnp.int32, (OWN, LANES), 1)
    row = lax.broadcasted_iota(jnp.int32, (OWN, LANES), 0)

    wide = lane[:PARTS]

    def record_window(shot):
        rows = [
            record_ref[:, piece * LANES : (piece + 1) * LANES]
            if RIM <= piece < OWN
            else jnp.zeros((PARTS, LANES), jnp.float32)
            for piece in range(shot, shot + RIM)
        ]
        for block, value in enumerate(read_windows(rows, own_ref[shot], wide)):
            window_ref[shot, :, block * LANES : (block + 1) * LANES] = 0.5 * value

    for half in range(2):
        traces = jnp.concatenate(
            [
                data[:, first : first + HALF, :].reshape(half_shots, LANES)
                for first in range(half * BLOCKS * HALF, (half + 1) * BLOCKS * HALF, HALF)
            ],
            axis=1,
        )
        real = dot(traces, full_ref[:, :FREQS]).astype(jnp.bfloat16)
        imag = (-dot(traces, full_ref[:, SHOTS : SHOTS + FREQS])).astype(jnp.bfloat16)
        stack_ref[half, :half_shots, :FREQS] = real
        stack_ref[half, :half_shots, FREQS:] = imag
        stack_ref[half, half_shots:, :FREQS] = imag
        stack_ref[half, half_shots:, FREQS:] = -real
        for shot in range(half * HALF, half * HALF + HALF):
            record_window(shot)

    waves = [dot(split_ref[half], stack_ref[half]) for half in range(2)]
    freq = lax.broadcasted_iota(jnp.int32, (1, FREQS), 1)
    weight = jnp.where(freq == 0, 1.0, 2.0).astype(jnp.float32)
    level = weight * threshold_ref[...]
    for half in range(2):
        fk = waves[0] + waves[1] if half == 0 else waves[0] - waves[1]
        real, imag = fk[:, :FREQS], fk[:, FREQS:]
        power = real * real + imag * imag + 1e-12
        factor = jnp.maximum(weight - level * lax.rsqrt(power), 0.0)
        less = (-imag * factor).astype(jnp.bfloat16)
        real = (real * factor).astype(jnp.bfloat16)
        here = slice(half * half_shots, (half + 1) * half_shots)
        there = slice(SHOTS + half * half_shots, SHOTS + (half + 1) * half_shots)
        shrunk_ref[here, :FREQS] = real
        shrunk_ref[there, :FREQS] = less
        shrunk_ref[here, FREQS:] = less
        shrunk_ref[there, FREQS:] = -real

    step = OWN

    def place(start):
        offset = offset_ref[start : start + step, :]
        index = (lane - offset) & (LANES - 1)
        near, far = lane >= offset, lane >= offset - LANES
        turned = [
            rotated(
                denoised_ref[start : start + step, block * LANES : (block + 1) * LANES], index
            )
            for block in range(BLOCKS)
        ]
        pieces = [
            jnp.where(near, turned[0], 0.0),
            jnp.where(near, turned[1], jnp.where(far, turned[0], 0.0)),
            jnp.where(near, turned[2], jnp.where(far, turned[1], turned[0])),
            jnp.where(near, turned[3], jnp.where(far, turned[2], turned[1])),
            jnp.where(near, 0.0, jnp.where(far, turned[3], turned[2])),
            jnp.where(far, 0.0, turned[3]),
        ]
        for at, piece in enumerate(pieces):
            placed_ref[at, 8 + start : 8 + start + step, :] = piece

    def subtract(start):
        total = placed_ref[0, 8 + start : 8 + start + step, :]
        for piece in range(1, RIM):
            total = total + placed_ref[piece, 8 + start - piece : 8 + start - piece + step, :]
        difference_ref[start : start + step, :] = -0.5 * total
        heads = data[start // step, BLOCKS * OWN : BLOCKS * OWN + 8, :].astype(jnp.float32)
        heads = jnp.where(row[:8] < RIM, 0.5 * heads, 0.0)
        difference_ref[start : start + 8, :] = difference_ref[start : start + 8, :] + heads

    def finish(start):
        offset = offset_ref[start : start + step, :]
        rows = [difference_ref[start + piece : start + piece + step, :] for piece in range(RIM)]
        for block, value in enumerate(read_windows(rows, offset, lane)):
            lanes = slice(block * LANES, (block + 1) * LANES)
            out_ref[start : start + step, lanes] = (
                denoised_ref[start : start + step, lanes] + value
            ).astype(jnp.bfloat16)

    for part in range(PARTS):
        rows = data[part, BLOCKS * OWN : BLOCKS * OWN + 8, :].astype(jnp.float32)
        rows = jnp.broadcast_to(rows[RIM + 1 :, :].astype(jnp.int32), (OWN, LANES))
        offset_ref[part * OWN : (part + 1) * OWN, :] = rotated(rows, row)

    inverse = jnp.concatenate([full_ref[:FREQS, :SHOTS], full_ref[:FREQS, SHOTS:]], axis=0)
    part_shots = SHOTS // CHUNKS
    steps = SHOTS // step
    subtracted, finished = 1, 1
    for part in range(CHUNKS):
        shots = slice(part * part_shots, (part + 1) * part_shots)
        back = dot(full_ref[shots, :], shrunk_ref[...]).astype(jnp.bfloat16)
        denoised_ref[shots, :] = dot(back[:, :FREQS], full_ref[:FREQS, :SHOTS]) + dot(
            back[:, FREQS:], full_ref[:FREQS, SHOTS:]
        )
        for start in range(part * part_shots, (part + 1) * part_shots, step):
            place(start)
        ready = (part + 1) * steps // CHUNKS
        for at in range(subtracted, ready):
            subtract(at * step)
        subtracted = ready
        for at in range(finished, ready - 1):
            finish(at * step)
        finished = ready - 1
    for piece in range(1, RIM):
        placed_ref[piece, 0:8, :] = placed_ref[piece, SHOTS : SHOTS + 8, :]
    subtract(0)
    difference_ref[SHOTS : SHOTS + 8, :] = difference_ref[0:8, :]
    finish(SHOTS - step)
    finish(0)


def unpack_kernel(data_ref, window_ref, out_hbm, out_ref, sems):
    width = NT // 2
    copies = []
    for half in range(2):
        shots = slice(half * HALF, (half + 1) * HALF)
        for side in range(2):
            lanes = slice(side * width, (side + 1) * width)
            rows = data_ref[:, shots, lanes]
            out_ref[shots, :, lanes] = (
                jnp.swapaxes(rows, 0, 1).astype(jnp.float32) + window_ref[shots, :, lanes]
            ).astype(jnp.bfloat16)
            place = (pl.ds(half * HALF, HALF), slice(None), pl.ds(side * width, width))
            copies.append(
                pltpu.make_async_copy(
                    out_ref.at[place], out_hbm.at[place], sems.at[2 * half + side]
                )
            )
            copies[-1].start()
    for copy in copies:
        copy.wait()


def vmem():
    return pl.BlockSpec(memory_space=pltpu.VMEM)


def hbm():
    return pl.BlockSpec(memory_space=pltpu.HBM)


def kept(value):
    return pltpu.with_memory_space_constraint(value, pltpu.HBM)


PARAMS = pltpu.CompilerParams(vmem_limit_bytes=VMEM_LIMIT)


def shards(estimate, record, fire_times, rcv_delay, threshold):
    packed, own, levels = pl.pallas_call(
        pack_kernel,
        out_shape=[
            jax.ShapeDtypeStruct((PARTS, PAYLOAD, LANES), jnp.bfloat16),
            jax.ShapeDtypeStruct((OWN, PARTS, LANES), jnp.int32),
            jax.ShapeDtypeStruct((1, FREQS), jnp.float32),
        ],
        in_specs=[hbm()] * 5,
        out_specs=[vmem()] * 3,
        scratch_shapes=[
            pltpu.SMEM((OWN,), jnp.int32),
            pltpu.SMEM((PARTS,), jnp.int32),
            pltpu.VMEM((2, HALF, PARTS, NT), jnp.bfloat16),
            pltpu.VMEM((PARTS, RIM * LANES), jnp.float32),
            pltpu.SemaphoreType.DMA((4,)),
            pltpu.SemaphoreType.DMA((2,)),
        ],
        compiler_params=PARAMS,
        name="pack",
    )(
        kept(fire_times),
        kept(rcv_delay),
        kept(estimate.reshape(HALF, 2, PARTS, NT)),
        kept(record),
        kept(threshold.reshape(1, FREQS)),
    )
    gathered = lax.all_to_all(packed, "shot", split_axis=0, concat_axis=0, tiled=True)
    split, full = (jnp.asarray(table) for table in tables())
    updated, window = pl.pallas_call(
        main_kernel,
        out_shape=[
            jax.ShapeDtypeStruct((SHOTS, NT), jnp.bfloat16),
            jax.ShapeDtypeStruct((OWN, PARTS, NT), jnp.float32),
        ],
        in_specs=[vmem()] * 6,
        out_specs=[vmem()] * 2,
        scratch_shapes=[
            pltpu.VMEM((2, SHOTS, NT), jnp.bfloat16),
            pltpu.VMEM((2 * SHOTS, NT), jnp.bfloat16),
            pltpu.VMEM((SHOTS, NT), jnp.float32),
            pltpu.VMEM((SHOTS, LANES), jnp.int32),
            pltpu.VMEM((RIM, SHOTS + 8, LANES), jnp.float32),
            pltpu.VMEM((SHOTS + 8, LANES), jnp.float32),
        ],
        compiler_params=PARAMS,
        name="main",
    )(
        levels,
        own,
        record,
        gathered,
        split,
        full,
    )
    returned = lax.all_to_all(
        updated.reshape(PARTS, OWN, NT), "shot", split_axis=0, concat_axis=0, tiled=True
    )
    return pl.pallas_call(
        unpack_kernel,
        out_shape=jax.ShapeDtypeStruct((OWN, PARTS, NT), jnp.bfloat16),
        in_specs=[vmem()] * 2,
        out_specs=hbm(),
        scratch_shapes=[
            pltpu.VMEM((OWN, PARTS, NT), jnp.bfloat16),
            pltpu.SemaphoreType.DMA((4,)),
        ],
        compiler_params=PARAMS,
        name="unpack",
    )(returned, window)


def solution(mesh):
    in_specs = (P("shot", "rcv", None), P("rcv", "shot"), P("shot"), P("rcv"), P())
    out_specs = P("shot", "rcv", None)
    return jax.shard_map(shards, mesh=mesh, in_specs=in_specs, out_specs=out_specs, check_vma=False)
```
